128 devices in a mesh: frame: 4 (over z), panel: 32 (over x, y, core).
Axes of the slice: x: 4, y: 4, z: 4, core: 2. Of those that a mesh axis runs over, the one named last changes fastest.
Arguments:
- spline_index: int32 [16384, 2, 4, 256], P(('frame', 'panel')), may hold values from 0 to 124
- spline_frac: bfloat16 [16384, 2, 4, 256], P(('frame', 'panel')), may hold values from 0 to 1
- projection: bfloat16 [16384, 2, 4, 256], P(('frame', 'panel')), may hold values from -6 to 6
- forces: bfloat16 [16384, 256], P(('frame', 'panel')), may hold values from -6 to 6
- row_owner: int32 [16384, 1], P(('frame', 'panel')), may hold values from 0 to 127, as said below
- row_offset: int32 [16384], P(('frame', 'panel')), may hold values from 0 to 21
Outputs:
- normal_band: float32 [2816, 2, 128, 128], P(('frame', 'panel'))
- normal_rhs: float32 [2816, 128], P(('frame', 'panel'))
The draws below stay inside these ranges and needn't reach their ends.
Inputs may be any that keep to these rules, and one draw needn't show every extreme that they name: `row_owner`: among the row tiles of one device, no owner index is named by more than 2 tiles, and some owner index is named by exactly 2. Every owner index is named by some row tile.
All inputs are finite; a program needn't handle non-finite values.
Results may differ from the reference program's by a relative error of at most 0.0029.
Values may be sent and summed in bfloat16 or wider, within the bound.
No kernel may reach another device: no remote copies, remote signals or barrier semaphores. Data moves between devices by JAX's collectives and lax.ppermute only.
A program may use at most 64 MiB of HBM per device.

```python
import jax
import jax.numpy as jnp
from jax import lax

CO = 128
BLK_DEV = 22
SLOTS = 2
NEI = 4
TR = 256
RT_DEV = 128
NBLK = 2816
ROWTILES = 16384
CAP = 2
DEVICES = 128


def draw_row_owner(key, part):
    rows = jnp.arange(ROWTILES, dtype=jnp.int32)
    device_of = rows // RT_DEV
    within = rows % RT_DEV
    shuffled = jax.random.permutation(jax.random.fold_in(key, 11), DEVICES).astype(jnp.int32)
    owner = (shuffled[device_of] + within // CAP) % DEVICES
    return owner[:, None].astype(jnp.int32)


def draw_row_offset(key, part):
    rows = jnp.arange(ROWTILES, dtype=jnp.int32)
    within = rows % RT_DEV
    drawn = jax.random.randint(jax.random.fold_in(key, 23), (ROWTILES,), 0, BLK_DEV, dtype=jnp.int32)
    return jnp.where(within % CAP == 0, BLK_DEV - 1, drawn).astype(jnp.int32)


def plant(entries, stream_key, smallest, top_value):
    index_at = [jax.random.randint(jax.random.fold_in(stream_key, axis), (), 0, length) for axis, length in enumerate(entries.shape)]
    main_axis = entries.shape.index(max(entries.shape))
    next_to = index_at[:main_axis] + [(index_at[main_axis] + 1) % entries.shape[main_axis]] + index_at[main_axis + 1:]
    return entries.at[tuple(index_at)].set(smallest).at[tuple(next_to)].set(top_value)


def levels(key, extent, cuts, smallest, top_value):
    loudness, own = 1.0, jax.random.fold_in(key, 6)
    for dim, blocks in cuts:
        draws = jnp.exp(jax.random.uniform(jax.random.fold_in(own, dim), (blocks,), jnp.float32, smallest / len(cuts), top_value / len(cuts)))
        loudness = loudness * jnp.repeat(draws, extent[dim] // blocks).reshape([-1 if axis == dim else 1 for axis in range(len(extent))])
    return loudness


def centred(stream_key, dims, scale, bound, cuts=(), kind=jnp.bfloat16):
    factor_of = levels(stream_key, dims, cuts, -0.22, 0.18) if cuts else 1.0
    array = jax.random.normal(stream_key, dims, jnp.float32) * scale * factor_of
    return jnp.minimum(jnp.maximum(array, -bound), bound).astype(kind)


def setup_inputs(seed: int = 0) -> dict:
    seeds = jax.random.split(jax.random.key(seed), 7)
    return {
        "spline_index": plant(jax.random.randint(seeds[0], (ROWTILES, SLOTS, NEI, TR), 0, CO - 3), jax.random.fold_in(seeds[0], 1), 0, (CO - 3) - 1).astype(jnp.int32),
        "spline_frac": jnp.clip(1.0 * jax.random.uniform(seeds[1], (ROWTILES, SLOTS, NEI, TR), jnp.float32) ** levels(seeds[1], (ROWTILES, SLOTS, NEI, TR), ((0, 128),), -0.2, 0.2), 0.0, 1.0).astype(jnp.bfloat16),
        "projection": centred(seeds[2], (ROWTILES, SLOTS, NEI, TR), 1.0, 6.0, ((0, 128),)),
        "forces": centred(seeds[3], (ROWTILES, TR), 1.0, 6.0, ((0, 128),)),
        "row_owner": draw_row_owner(jax.random.fold_in(seeds[6], 71), 0),
        "row_offset": draw_row_offset(jax.random.fold_in(seeds[6], 71), 0),
    }


def basis_tiles(spline_index, spline_frac, projection, column_count):
    columns = lax.broadcasted_iota(jnp.int32, (1, 1, 1, column_count), 3)
    summed = jnp.zeros(spline_index.shape[:2] + (spline_index.shape[3], column_count), jnp.float32)
    for neighbor in range(spline_index.shape[2]):
        offset = columns - spline_index[:, :, neighbor, :, None]
        position = spline_frac[:, :, neighbor, :, None].astype(jnp.float32)
        weight = projection[:, :, neighbor, :, None].astype(jnp.float32)
        one_minus = 1.0 - position
        pos_square = position * position
        pos_cube = pos_square * position
        basis_zero = one_minus * one_minus * one_minus / 6.0
        basis_one = (3.0 * pos_cube - 6.0 * pos_square + 4.0) / 6.0
        basis_two = (-3.0 * pos_cube + 3.0 * pos_square + 3.0 * position + 1.0) / 6.0
        basis_three = pos_cube / 6.0
        basis_value = jnp.where(offset == 0, basis_zero,
                      jnp.where(offset == 1, basis_one,
                      jnp.where(offset == 2, basis_two,
                      jnp.where(offset == 3, basis_three, 0.0))))
        summed = summed + weight * basis_value
    return summed.astype(jnp.bfloat16)


def reference(spline_index, spline_frac, projection, forces, row_owner, row_offset):
    total_rows = spline_index.shape[0]
    slot_width = spline_index.shape[1]
    start = (row_owner[:, 0] * BLK_DEV + row_offset).astype(jnp.int32)
    batch_size = 256 if total_rows % 256 == 0 else total_rows
    turns = total_rows // batch_size

    def split(member):
        return member.reshape((turns, batch_size) + member.shape[1:])

    def accumulate(totals, pieces):
        band_acc, rhs_acc = totals
        index_part, frac_part, proj_part, force_part, start_part = pieces
        design = basis_tiles(index_part, frac_part, proj_part, CO).astype(jnp.float32)
        for band_lag in range(slot_width):
            left_tiles = design[:, :slot_width - band_lag]
            right_tiles = design[:, band_lag:]
            products = jnp.einsum("bsxi,bsxj->bsij", left_tiles, right_tiles,
                                  precision=lax.Precision.HIGHEST)
            rows_at = (start_part[:, None] + jnp.arange(slot_width - band_lag, dtype=jnp.int32)[None, :]) % NBLK
            band_acc = band_acc.at[rows_at, band_lag].add(products)
        moments = jnp.einsum("bsxi,bx->bsi", design, force_part.astype(jnp.float32),
                             precision=lax.Precision.HIGHEST)
        rows_all = (start_part[:, None] + jnp.arange(slot_width, dtype=jnp.int32)[None, :]) % NBLK
        rhs_acc = rhs_acc.at[rows_all].add(moments)
        return (band_acc, rhs_acc), None

    band_init = jnp.zeros((NBLK, slot_width, CO, CO), jnp.float32)
    rhs_init = jnp.zeros((NBLK, CO), jnp.float32)
    (normal_band, normal_rhs), unused = lax.scan(
        accumulate, (band_init, rhs_init),
        (split(spline_index), split(spline_frac), split(projection), split(forces), split(start)))
    return normal_band, normal_rhs
```

```python
import jax
import jax.numpy as jnp
from jax import lax
from jax.experimental import pallas as pl
from jax.experimental.pallas import tpu as pltpu
from jax.sharding import PartitionSpec as P

CO = 128
BLK_DEV = 22
CAP = 2
AXES = ("frame", "panel")
BF16 = jnp.bfloat16
F32 = jnp.float32


def pack_kernel(owner_ref, index_ref, frac_ref, proj_ref, force_ref, out_ref, count_ref, force_buf):
    device_count = out_ref.shape[0]

    @pl.loop(0, device_count)
    def _(d):
        count_ref[d] = 0

    force_buf[...] = force_ref[...].astype(F32)

    @pl.loop(0, owner_ref.shape[0])
    def _(t):
        owner = owner_ref[t]
        place = count_ref[owner]
        count_ref[owner] = place + 1
        for a, ref in enumerate((index_ref, frac_ref, proj_ref)):
            for g in range(2):
                low = ref[t, 0, :, g * 128 : g * 128 + 128].astype(F32)
                high = ref[t, 1, :, g * 128 : g * 128 + 128].astype(F32)
                both = jnp.concatenate([low, high], axis=0).astype(BF16)
                out_ref[owner, place * 6 + a * 2 + g] = both

        row = force_buf[pl.ds(t, 1), :]
        for g in range(2):
            piece = jnp.broadcast_to(row[:, g * 128 : g * 128 + 128], (8, 128)).astype(BF16)
            which = lax.broadcasted_iota(jnp.int32, (8, 128), 0)
            old = out_ref[owner, 12]
            out_ref[owner, 12] = jnp.where(which == place * 2 + g, piece.astype(F32), old.astype(F32)).astype(BF16)


def pack(owners, spline_index, spline_frac, projection, forces, device_count):
    vmem = pl.BlockSpec(memory_space=pltpu.VMEM)
    return pl.pallas_call(
        pack_kernel,
        out_shape=jax.ShapeDtypeStruct((device_count, 13, 8, 128), BF16),
        in_specs=[pl.BlockSpec(memory_space=pltpu.SMEM), vmem, vmem, vmem, vmem],
        out_specs=vmem,
        scratch_shapes=[pltpu.SMEM((device_count,), jnp.int32), pltpu.VMEM(forces.shape, F32)],
        compiler_params=pltpu.CompilerParams(vmem_limit_bytes=40 << 20),
        name="pack",
    )(owners, spline_index, spline_frac, projection, forces)


def spline_rows(recv_ref, source, place, value_buf):
    for g in range(2):
        index = recv_ref[source, place * 6 + g].astype(F32).astype(jnp.int32)
        t = recv_ref[source, place * 6 + 2 + g].astype(F32)
        q = recv_ref[source, place * 6 + 4 + g].astype(F32) * (1.0 / 6.0)
        u = 1.0 - t
        t2 = t * t
        value_buf[0, g] = q * (u * u * u)
        value_buf[1, g] = q * (3.0 * (t2 * t) - 6.0 * t2 + 4.0)
        value_buf[2, g] = q * (3.0 * (t + t2 - t2 * t) + 1.0)
        value_buf[3, g] = q * (t2 * t)
        value_buf[4, g] = (index & 15).astype(F32)
        value_buf[5, g] = (index >> 4).astype(F32)


def build_design(value_buf, design_buf):
    column = lax.broadcasted_iota(jnp.int32, (16, 128), 0).astype(F32).astype(BF16)
    zero = jnp.zeros((16, 128), BF16)

    def spread(k, row, g):
        part = value_buf[k, g, pl.ds(row, 8, stride=0), :]
        return jnp.concatenate([part, part], axis=0).astype(BF16)

    for s in range(2):
        for g in range(2):
            blocks = [None] * 8
            for n in range(4):
                row = s * 4 + n
                low = spread(4, row, g)
                high = spread(5, row, g)
                offset = column - low
                wraps = offset < 0
                offset = jnp.where(wraps, offset + 16, offset)
                home = jnp.where(wraps, high + 1, high)
                window = zero
                for m in range(4):
                    window = jnp.where(offset == m, spread(m, row, g), window)
                for b in range(8):
                    piece = jnp.where(home == b, window, zero)
                    blocks[b] = piece if n == 0 else blocks[b] + piece
            for b in range(8):
                design_buf[s * 128 + b * 16 : s * 128 + b * 16 + 16, g * 128 : g * 128 + 128] = blocks[b]


def force_rows(recv_ref, source, place, design_buf, force_buf):
    force_buf[...] = recv_ref[source, 12].astype(F32)
    first = lax.broadcasted_iota(jnp.int32, (16, 128), 0) == 0
    for g in range(2):
        row = force_buf[pl.ds(place * 2 + g, 8, stride=0), :]
        row = jnp.concatenate([row, row], axis=0)
        design_buf[256:272, g * 128 : g * 128 + 128] = jnp.where(first, row, 0.0).astype(BF16)


def tile_products(recv_ref, code, value_buf, design_buf, force_buf):
    source = code >> 1
    place = code & 1
    spline_rows(recv_ref, source, place, value_buf)
    build_design(value_buf, design_buf)
    force_rows(recv_ref, source, place, design_buf, force_buf)
    return lax.dot_general(
        design_buf[...], design_buf[0:256, :], (((1,), (1,)), ((), ())), preferred_element_type=F32
    )


def edge_kernel(bounds_ref, order_ref, recv_ref, band_ref, rhs_ref, spill_ref, value_buf, design_buf, force_buf):
    band_ref[...] = jnp.zeros_like(band_ref)
    rhs_ref[...] = jnp.zeros_like(rhs_ref)
    spill_ref[...] = jnp.zeros_like(spill_ref)

    @pl.loop(0, bounds_ref[0])
    def _(i):
        out = tile_products(recv_ref, order_ref[i], value_buf, design_buf, force_buf)
        band_ref[0] += out[0:128, 0:128]
        band_ref[1] += out[0:128, 128:256]
        spill_ref[0:128, :] += out[128:256, 128:256]
        rhs_ref[...] += out[256:264, 0:128]
        spill_ref[128:136, :] += out[256:264, 128:256]


def inner_kernel(
    bounds_ref, order_ref, offset_ref, recv_ref, edge_band_ref, edge_rhs_ref, band_ref, rhs_ref,
    value_buf, design_buf, force_buf,
):
    last = band_ref.shape[0] - 1
    band_ref[0:last] = jnp.zeros((last, 2, 128, 128), F32)
    band_ref[last] = edge_band_ref[...]
    rhs_ref[0:last] = jnp.zeros((last, 128), F32)
    rhs_ref[last:last + 1] = edge_rhs_ref[0:1, :]

    @pl.loop(bounds_ref[0], bounds_ref[1])
    def _(i):
        out = tile_products(recv_ref, order_ref[i], value_buf, design_buf, force_buf)
        at = offset_ref[i]
        band_ref[at, 0] += out[0:128, 0:128]
        band_ref[at, 1] += out[0:128, 128:256]
        band_ref[at + 1, 0] += out[128:256, 128:256]
        rhs_ref[pl.ds(at, 1), :] += out[256:257, 0:128]
        rhs_ref[pl.ds(at + 1, 1), :] += out[256:257, 128:256]


SCRATCH = (
    pltpu.VMEM((6, 2, 8, 128), F32),
    pltpu.VMEM((272, 256), BF16),
    pltpu.VMEM((8, 128), F32),
)


def edge(bounds, order, received):
    vmem = pl.BlockSpec(memory_space=pltpu.VMEM)
    smem = pl.BlockSpec(memory_space=pltpu.SMEM)
    return pl.pallas_call(
        edge_kernel,
        out_shape=(
            jax.ShapeDtypeStruct((2, 128, 128), F32),
            jax.ShapeDtypeStruct((8, 128), F32),
            jax.ShapeDtypeStruct((136, 128), F32),
        ),
        in_specs=[smem, smem, vmem],
        out_specs=(vmem, vmem, vmem),
        scratch_shapes=list(SCRATCH),
        compiler_params=pltpu.CompilerParams(vmem_limit_bytes=40 << 20),
        cost_estimate=pl.CostEstimate(flops=4 << 30, bytes_accessed=4 << 20, transcendentals=0),
        name="edge",
    )(bounds, order, received)


def inner(bounds, order, offsets, received, edge_band, edge_rhs):
    vmem = pl.BlockSpec(memory_space=pltpu.VMEM)
    smem = pl.BlockSpec(memory_space=pltpu.SMEM)
    return pl.pallas_call(
        inner_kernel,
        out_shape=(
            jax.ShapeDtypeStruct((BLK_DEV, 2, 128, 128), F32),
            jax.ShapeDtypeStruct((BLK_DEV, 128), F32),
        ),
        in_specs=[smem, smem, smem, vmem, vmem, vmem],
        out_specs=(vmem, vmem),
        scratch_shapes=list(SCRATCH),
        compiler_params=pltpu.CompilerParams(vmem_limit_bytes=40 << 20),
        cost_estimate=pl.CostEstimate(flops=4 << 30, bytes_accessed=4 << 20, transcendentals=0),
        name="inner",
    )(bounds, order, offsets, received, edge_band, edge_rhs)


def work_list(all_owners, all_offsets, me):
    mine = all_owners == me
    before = jnp.cumsum(mine.astype(jnp.int32), axis=1)
    columns = []
    for place in range(CAP):
        here = mine & (before == place + 1)
        columns.append(jnp.sum(jnp.where(here, all_offsets + 1, 0), axis=1))
    slot_offset = jnp.stack(columns, axis=1).reshape(-1) - 1
    count = slot_offset.shape[0]
    key = jnp.where(slot_offset < 0, BLK_DEV, jnp.where(slot_offset == BLK_DEV - 1, -1, slot_offset))
    ahead = lax.broadcasted_iota(jnp.int32, (count, count), 1) < lax.broadcasted_iota(jnp.int32, (count, count), 0)
    smaller = (key[None, :] < key[:, None]) | ((key[None, :] == key[:, None]) & ahead)
    rank = jnp.sum(smaller.astype(jnp.int32), axis=1)
    chosen = rank[None, :] == lax.broadcasted_iota(jnp.int32, (count, count), 0)
    order = jnp.sum(jnp.where(chosen, lax.broadcasted_iota(jnp.int32, (count, count), 1), 0), axis=1)
    offsets = jnp.sum(jnp.where(chosen, slot_offset[None, :], 0), axis=1)
    bounds = jnp.stack([jnp.sum((slot_offset == BLK_DEV - 1).astype(jnp.int32)), jnp.sum((slot_offset >= 0).astype(jnp.int32))])
    return bounds, order, offsets


def on_device(spline_index, spline_frac, projection, forces, row_owner, row_offset):
    device_count = lax.axis_size(AXES)
    owners = row_owner[:, 0]
    sent = pack(owners, spline_index, spline_frac, projection, forces, device_count)
    received = lax.all_to_all(sent, AXES, split_axis=0, concat_axis=0, tiled=True)
    meta = lax.all_gather(jnp.stack([owners, row_offset]), AXES)
    bounds, order, offsets = work_list(meta[:, 0], meta[:, 1], lax.axis_index(AXES))
    edge_band, edge_rhs, spill = edge(bounds, order, received)
    route = [(i, (i + 1) % device_count) for i in range(device_count)]
    spill = lax.ppermute(spill, AXES, route)
    band, rhs = inner(bounds, order, offsets, received, edge_band, edge_rhs)
    band = band.at[0, 0].add(spill[0:128])
    rhs = rhs.at[0].add(spill[128])
    return band, rhs


def solution(mesh):
    in_specs = (
        P(AXES, None, None, None),
        P(AXES, None, None, None),
        P(AXES, None, None, None),
        P(AXES, None),
        P(AXES, None),
        P(AXES),
    )
    out_specs = (P(AXES, None, None, None), P(AXES, None))
    return jax.shard_map(
        on_device, mesh=mesh, in_specs=in_specs, out_specs=out_specs, check_vma=False
    )
```

```python
import jax
import jax.numpy as jnp
from jax import lax
from jax.experimental import pallas as pl
from jax.experimental.pallas import tpu as pltpu
from jax.sharding import PartitionSpec as P

CO = 128
BLK_DEV = 22
CAP = 2
AXES = ("frame", "panel")
BF16 = jnp.bfloat16
F32 = jnp.float32
CHUNKS = 8
MiB = 1 << 20


def pack_kernel(
    owner_ref, offset_ref, me_ref, index_hbm, frac_hbm, proj_hbm, force_hbm, out_hbm,
    count_ref, index_ref, frac_ref, proj_ref, force_ref, force_f32, tile_ref, tail_f32, tail_ref,
    in_sems, force_sem, out_sem, tail_sem,
):
    device_count = out_hbm.shape[0]
    tiles = owner_ref.shape[0]
    step = tiles // CHUNKS
    arrays = ((index_hbm, index_ref), (frac_hbm, frac_ref), (proj_hbm, proj_ref))

    def fetch(a, c):
        part = pl.ds(c * step, step)
        return pltpu.make_async_copy(arrays[a][0].at[part], arrays[a][1].at[part], in_sems.at[a, c])

    force_copy = pltpu.make_async_copy(force_hbm, force_ref, force_sem)
    force_copy.start()
    for c in range(CHUNKS):
        for a in range(3):
            fetch(a, c).start()

    @pl.loop(0, device_count, unroll=8)
    def _(d):
        count_ref[d] = 0

    tail_f32[...] = jnp.zeros_like(tail_f32)
    here = lax.broadcasted_iota(jnp.int32, (1, 128), 1) == me_ref[0]
    force_copy.wait()
    force_f32[...] = force_ref[...].astype(F32)

    for c in range(CHUNKS):
        for a in range(3):
            fetch(a, c).wait()

        @pl.loop(c * step, (c + 1) * step, unroll=2)
        def _(t):
            owner = owner_ref[t]
            place = count_ref[owner]
            count_ref[owner] = place + 1
            for a in range(3):
                ref = arrays[a][1]
                for g in range(2):
                    low = ref[t, 0, :, g * 128 : g * 128 + 128].astype(F32)
                    high = ref[t, 1, :, g * 128 : g * 128 + 128].astype(F32)
                    tile_ref[t, a * 2 + g] = jnp.concatenate([low, high], axis=0).astype(BF16)
            pltpu.make_async_copy(tile_ref.at[t], out_hbm.at[owner, pl.ds(place * 6, 6)], out_sem).start()
            row = force_f32[pl.ds(t, 1), :]
            for g in range(2):
                tail_f32[owner, pl.ds(place * 2 + g, 1), :] = row[:, g * 128 : g * 128 + 128]
            tail_f32[owner, pl.ds(4 + place, 1), :] = jnp.where(here, (offset_ref[t] + 1).astype(F32), 0.0)

    tail_ref[...] = tail_f32[...].astype(BF16)
    tail_copy = pltpu.make_async_copy(tail_ref, out_hbm.at[:, 12], tail_sem)
    tail_copy.start()
    tail_copy.wait()
    pltpu.make_async_copy(tile_ref, tile_ref, out_sem).wait()


def pack(owners, offsets, me, spline_index, spline_frac, projection, forces, device_count):
    hbm = pl.BlockSpec(memory_space=pltpu.HBM)
    smem = pl.BlockSpec(memory_space=pltpu.SMEM)
    tiles = owners.shape[0]
    return pl.pallas_call(
        pack_kernel,
        out_shape=jax.ShapeDtypeStruct((device_count, 13, 8, 128), BF16),
        in_specs=[smem, smem, smem, hbm, hbm, hbm, hbm],
        out_specs=hbm,
        scratch_shapes=[
            pltpu.SMEM((device_count,), jnp.int32),
            pltpu.VMEM(spline_index.shape, spline_index.dtype),
            pltpu.VMEM(spline_frac.shape, BF16),
            pltpu.VMEM(projection.shape, BF16),
            pltpu.VMEM(forces.shape, BF16),
            pltpu.VMEM(forces.shape, F32),
            pltpu.VMEM((tiles, 6, 8, 128), BF16),
            pltpu.VMEM((device_count, 8, 128), F32),
            pltpu.VMEM((device_count, 8, 128), BF16),
            pltpu.SemaphoreType.DMA((3, CHUNKS)),
            pltpu.SemaphoreType.DMA,
            pltpu.SemaphoreType.DMA,
            pltpu.SemaphoreType.DMA,
        ],
        compiler_params=pltpu.CompilerParams(vmem_limit_bytes=40 * MiB),
        name="pack",
    )(owners, offsets, me, spline_index, spline_frac, projection, forces)


def spline_rows(recv_ref, source, place, scale, value_buf):
    for g in range(2):
        index = recv_ref[source, place * 6 + g].astype(F32).astype(jnp.int32)
        t = recv_ref[source, place * 6 + 2 + g].astype(F32)
        q = recv_ref[source, place * 6 + 4 + g].astype(F32) * scale
        u = 1.0 - t
        t2 = t * t
        t3 = t2 * t
        value_buf[0, g] = q * (u * u * u)
        value_buf[1, g] = q * (3.0 * t3 - 6.0 * t2 + 4.0)
        value_buf[2, g] = q * (3.0 * (t + t2 - t3) + 1.0)
        value_buf[3, g] = q * t3
        value_buf[4, g] = (index & 15).astype(F32)
        value_buf[5, g] = (index >> 4).astype(F32)


def build_design(value_buf, design_buf):
    column = lax.broadcasted_iota(jnp.int32, (16, 128), 0).astype(F32).astype(BF16)
    zero = jnp.zeros((16, 128), BF16)

    def spread(k, row, g):
        part = value_buf[k, g, pl.ds(row, 8, stride=0), :]
        return jnp.concatenate([part, part], axis=0).astype(BF16)

    for s in range(2):
        for g in range(2):
            blocks = [None] * 8
            for n in range(4):
                row = s * 4 + n
                low = spread(4, row, g)
                high = spread(5, row, g)
                offset = column - low
                wraps = offset < 0
                offset = jnp.where(wraps, offset + 16, offset)
                home = jnp.where(wraps, high + 1, high)
                window = zero
                for m in range(4):
                    window = jnp.where(offset == m, spread(m, row, g), window)
                for b in range(8):
                    piece = jnp.where(home == b, window, zero)
                    blocks[b] = piece if n == 0 else blocks[b] + piece
            for b in range(8):
                design_buf[s * 128 + b * 16 : s * 128 + b * 16 + 16, g * 128 : g * 128 + 128] = blocks[b]


def force_rows(recv_ref, source, place, design_buf, force_buf):
    force_buf[...] = recv_ref[source, 12].astype(F32)
    first = lax.broadcasted_iota(jnp.int32, (16, 128), 0) == 0
    for g in range(2):
        row = force_buf[pl.ds(place * 2 + g, 8, stride=0), :]
        row = jnp.concatenate([row, row], axis=0)
        design_buf[256:272, g * 128 : g * 128 + 128] = jnp.where(first, row, 0.0).astype(BF16)


def build_tile(recv_ref, code, scale, bufs):
    value_buf, design_buf, force_buf = bufs
    source = code >> 1
    place = code & 1
    spline_rows(recv_ref, source, place, scale, value_buf)
    force_rows(recv_ref, source, place, design_buf, force_buf)
    build_design(value_buf, design_buf)


def products(design_buf):
    return lax.dot_general(
        design_buf[...], design_buf[0:256, :], (((1,), (1,)), ((), ())), preferred_element_type=F32
    )


def sweep(first, last, code_at, recv_ref, add, even, odd):
    odd[1][...] = jnp.zeros_like(odd[1])

    def pair(j, carry):
        i = first + 2 * j
        add(jnp.maximum(i - 1, first), products(odd[1]))
        build_tile(recv_ref, code_at(i), 1.0 / 6.0, even)
        add(i, products(even[1]))
        after = jnp.minimum(i + 1, last - 1)
        build_tile(recv_ref, code_at(after), jnp.where(i + 1 < last, 1.0 / 6.0, 0.0).astype(F32), odd)
        return carry

    lax.fori_loop(0, (last - first + 1) // 2, pair, 0)

    @pl.when(last > first)
    def _():
        add(last - 1, products(odd[1]))


def edge_kernel(recv_ref, band_ref, rhs_ref, spill_ref, list_ref, bound_ref, meta_f32, meta_i32, meta_ref, meta_sem, *bufs):
    total = jnp.zeros((8, 128), F32)
    for d in range(recv_ref.shape[0]):
        total = total + recv_ref[d, 12].astype(F32)
    meta_i32[...] = total.astype(jnp.int32)
    meta_copy = pltpu.make_async_copy(meta_i32, meta_ref, meta_sem)
    meta_copy.start()
    band_ref[...] = jnp.zeros_like(band_ref)
    rhs_ref[...] = jnp.zeros_like(rhs_ref)
    spill_ref[...] = jnp.zeros_like(spill_ref)
    meta_copy.wait()

    def scan(d, counts):
        edges, others = counts
        for q in range(CAP):
            mark = meta_ref[4 + q, d]
            list_ref[0, edges] = d * CAP + q
            edges = edges + (mark == BLK_DEV).astype(jnp.int32)
            list_ref[1, others] = d * CAP + q
            list_ref[2, others] = mark - 1
            others = others + ((mark > 0) & (mark < BLK_DEV)).astype(jnp.int32)
        return edges, others

    edges, others = lax.fori_loop(0, recv_ref.shape[0], scan, (0, 0), unroll=8)
    bound_ref[0] = others

    def add(i, out):
        band_ref[0] += out[0:128, 0:128]
        band_ref[1] += out[0:128, 128:256]
        spill_ref[0:128, :] += out[128:256, 128:256]
        rhs_ref[...] += out[256:264, 0:128]
        spill_ref[128:136, :] += out[256:264, 128:256]

    sweep(0, edges, lambda i: list_ref[0, i], recv_ref, add, bufs[0:3], bufs[3:6])


def inner_kernel(bound_ref, list_ref, recv_ref, edge_band_ref, edge_rhs_ref, band_ref, rhs_ref, *bufs):
    last = band_ref.shape[0] - 1
    band_ref[0:last] = jnp.zeros((last, 2, 128, 128), F32)
    band_ref[last] = edge_band_ref[...]
    rhs_ref[0:last] = jnp.zeros((last, 128), F32)
    rhs_ref[last:last + 1] = edge_rhs_ref[0:1, :]

    def add(i, out):
        at = list_ref[2, i]
        band_ref[at, 0] += out[0:128, 0:128]
        band_ref[at, 1] += out[0:128, 128:256]
        band_ref[at + 1, 0] += out[128:256, 128:256]
        rhs_ref[pl.ds(at, 1), :] += out[256:257, 0:128]
        rhs_ref[pl.ds(at + 1, 1), :] += out[256:257, 128:256]

    sweep(0, bound_ref[0], lambda i: list_ref[1, i], recv_ref, add, bufs[0:3], bufs[3:6])


def buffers():
    return [pltpu.VMEM((6, 2, 8, 128), F32), pltpu.VMEM((272, 256), BF16), pltpu.VMEM((8, 128), F32)] * 2


def edge(received):
    vmem = pl.BlockSpec(memory_space=pltpu.VMEM)
    smem = pl.BlockSpec(memory_space=pltpu.SMEM)
    slots = received.shape[0] * CAP
    return pl.pallas_call(
        edge_kernel,
        out_shape=(
            jax.ShapeDtypeStruct((2, 128, 128), F32),
            jax.ShapeDtypeStruct((8, 128), F32),
            jax.ShapeDtypeStruct((136, 128), F32),
            jax.ShapeDtypeStruct((3, slots + 1), jnp.int32),
            jax.ShapeDtypeStruct((1,), jnp.int32),
        ),
        in_specs=[vmem],
        out_specs=(vmem, vmem, vmem, smem, smem),
        scratch_shapes=[
            pltpu.VMEM((8, 128), F32),
            pltpu.VMEM((8, 128), jnp.int32),
            pltpu.SMEM((8, 128), jnp.int32),
            pltpu.SemaphoreType.DMA,
        ]
        + buffers(),
        compiler_params=pltpu.CompilerParams(vmem_limit_bytes=40 * MiB),
        cost_estimate=pl.CostEstimate(flops=4 << 30, bytes_accessed=4 << 20, transcendentals=0),
        name="edge",
    )(received)


def inner(bound, lists, received, edge_band, edge_rhs):
    vmem = pl.BlockSpec(memory_space=pltpu.VMEM)
    smem = pl.BlockSpec(memory_space=pltpu.SMEM)
    return pl.pallas_call(
        inner_kernel,
        out_shape=(
            jax.ShapeDtypeStruct((BLK_DEV, 2, 128, 128), F32),
            jax.ShapeDtypeStruct((BLK_DEV, 128), F32),
        ),
        in_specs=[smem, smem, vmem, vmem, vmem],
        out_specs=(vmem, vmem),
        scratch_shapes=buffers(),
        compiler_params=pltpu.CompilerParams(vmem_limit_bytes=40 * MiB),
        cost_estimate=pl.CostEstimate(flops=4 << 30, bytes_accessed=4 << 20, transcendentals=0),
        name="inner",
    )(bound, lists, received, edge_band, edge_rhs)


def on_device(spline_index, spline_frac, projection, forces, row_owner, row_offset):
    device_count = lax.axis_size(AXES)
    me = lax.axis_index(AXES).astype(jnp.int32).reshape(1)
    sent = pack(row_owner[:, 0], row_offset, me, spline_index, spline_frac, projection, forces, device_count)
    received = lax.all_to_all(sent, AXES, split_axis=0, concat_axis=0, tiled=True)
    edge_band, edge_rhs, spill, lists, bound = edge(received)
    route = [(i, (i + 1) % device_count) for i in range(device_count)]
    spill = lax.ppermute(spill, AXES, route)
    band, rhs = inner(bound, lists, received, edge_band, edge_rhs)
    band = band.at[0, 0].add(spill[0:128])
    rhs = rhs.at[0].add(spill[128])
    return band, rhs


def solution(mesh):
    in_specs = (
        P(AXES, None, None, None),
        P(AXES, None, None, None),
        P(AXES, None, None, None),
        P(AXES, None),
        P(AXES, None),
        P(AXES),
    )
    out_specs = (P(AXES, None, None, None), P(AXES, None))
    return jax.shard_map(
        on_device, mesh=mesh, in_specs=in_specs, out_specs=out_specs, check_vma=False
    )
```

```python
import jax
import jax.numpy as jnp
from jax import lax
from jax.experimental import pallas as pl
from jax.experimental.pallas import tpu as pltpu
from jax.sharding import PartitionSpec as P

CO = 128
BLK_DEV = 22
CAP = 2
AXES = ("frame", "panel")
BF16 = jnp.bfloat16
F32 = jnp.float32
CHUNKS = 8
MiB = 1 << 20


def pack_kernel(
    owner_ref, offset_ref, me_ref, index_hbm, frac_hbm, proj_hbm, force_hbm, out_hbm,
    count_ref, index_ref, frac_ref, proj_ref, force_ref, force_f32, tile_ref, tail_f32, tail_ref,
    in_sems, force_sem, out_sem, tail_sem,
):
    device_count = out_hbm.shape[0]
    tiles = owner_ref.shape[0]
    step = tiles // CHUNKS
    arrays = ((index_hbm, index_ref), (frac_hbm, frac_ref), (proj_hbm, proj_ref))

    def fetch(a, c):
        part = pl.ds(c * step, step)
        return pltpu.make_async_copy(arrays[a][0].at[part], arrays[a][1].at[part], in_sems.at[a, c])

    force_copy = pltpu.make_async_copy(force_hbm, force_ref, force_sem)
    force_copy.start()
    for c in range(CHUNKS):
        for a in range(3):
            fetch(a, c).start()

    @pl.loop(0, device_count, unroll=8)
    def _(d):
        count_ref[d] = 0

    tail_f32[...] = jnp.zeros_like(tail_f32)
    here = lax.broadcasted_iota(jnp.int32, (1, 128), 1) == me_ref[0]
    force_copy.wait()
    force_f32[...] = force_ref[...].astype(F32)

    for c in range(CHUNKS):
        for a in range(3):
            fetch(a, c).wait()

        @pl.loop(c * step, (c + 1) * step, unroll=2)
        def _(t):
            owner = owner_ref[t]
            place = count_ref[owner]
            count_ref[owner] = place + 1
            for a in range(3):
                ref = arrays[a][1]
                for g in range(2):
                    low = ref[t, 0, :, g * 128 : g * 128 + 128].astype(F32)
                    high = ref[t, 1, :, g * 128 : g * 128 + 128].astype(F32)
                    tile_ref[t, a * 2 + g] = jnp.concatenate([low, high], axis=0).astype(BF16)
            pltpu.make_async_copy(tile_ref.at[t], out_hbm.at[owner, pl.ds(place * 6, 6)], out_sem).start()
            row = force_f32[pl.ds(t, 1), :]
            for g in range(2):
                tail_f32[owner, pl.ds(place * 2 + g, 1), :] = row[:, g * 128 : g * 128 + 128]
            tail_f32[owner, pl.ds(4 + place, 1), :] = jnp.where(here, (offset_ref[t] + 1).astype(F32), 0.0)

    tail_ref[...] = tail_f32[...].astype(BF16)
    tail_copy = pltpu.make_async_copy(tail_ref, out_hbm.at[:, 12], tail_sem)
    tail_copy.start()
    tail_copy.wait()
    pltpu.make_async_copy(tile_ref, tile_ref, out_sem).wait()


def pack(owners, offsets, me, spline_index, spline_frac, projection, forces, device_count):
    hbm = pl.BlockSpec(memory_space=pltpu.HBM)
    smem = pl.BlockSpec(memory_space=pltpu.SMEM)
    tiles = owners.shape[0]
    return pl.pallas_call(
        pack_kernel,
        out_shape=jax.ShapeDtypeStruct((device_count, 13, 8, 128), BF16),
        in_specs=[smem, smem, smem, hbm, hbm, hbm, hbm],
        out_specs=hbm,
        scratch_shapes=[
            pltpu.SMEM((device_count,), jnp.int32),
            pltpu.VMEM(spline_index.shape, spline_index.dtype),
            pltpu.VMEM(spline_frac.shape, BF16),
            pltpu.VMEM(projection.shape, BF16),
            pltpu.VMEM(forces.shape, BF16),
            pltpu.VMEM(forces.shape, F32),
            pltpu.VMEM((tiles, 6, 8, 128), BF16),
            pltpu.VMEM((device_count, 8, 128), F32),
            pltpu.VMEM((device_count, 8, 128), BF16),
            pltpu.SemaphoreType.DMA((3, CHUNKS)),
            pltpu.SemaphoreType.DMA,
            pltpu.SemaphoreType.DMA,
            pltpu.SemaphoreType.DMA,
        ],
        compiler_params=pltpu.CompilerParams(vmem_limit_bytes=60 * MiB),
        name="pack",
    )(owners, offsets, me, spline_index, spline_frac, projection, forces)


def spline_rows(recv_ref, source, place, scale, bufs):
    base_buf, window_buf = bufs[0:2]
    pieces = [[], [], [], []]
    lows = []
    for g in range(2):
        index = recv_ref[source, place * 6 + g].astype(F32)
        t = recv_ref[source, place * 6 + 2 + g].astype(F32)
        q = recv_ref[source, place * 6 + 4 + g].astype(F32) * scale
        base_buf[g] = index * (1.0 / 16.0)
        lows.append((index.astype(jnp.int32) & 15).astype(F32))
        u = 1.0 - t
        t2 = t * t
        t3 = t2 * t
        pieces[0].append(q * (u * u * u))
        pieces[1].append(q * (3.0 * t3 - 6.0 * t2 + 4.0))
        pieces[2].append(q * (3.0 * (t + t2 - t3) + 1.0))
        pieces[3].append(q * t3)
    low = jnp.concatenate(lows, axis=0).astype(BF16)
    pieces = [jnp.concatenate(p, axis=0).astype(BF16) for p in pieces]
    starts = [low == k for k in range(16)]
    zero = jnp.zeros((16, 128), BF16)
    for k in range(16):
        value = zero
        for m in range(4):
            value = jnp.where(starts[(k - m) % 16], pieces[m], value)
        value = value.astype(F32)
        for g in range(2):
            window_buf[g, pl.ds(k, 8, stride=24), :] = value[g * 8 : g * 8 + 8]


def build_design(bufs):
    base_buf, window_buf, design_buf = bufs[0:3]
    shift = (lax.broadcasted_iota(jnp.int32, (16, 128), 0).astype(F32) * (1.0 / 16.0) - 7.5 / 16.0).astype(BF16)
    zero = jnp.zeros((16, 128), BF16)
    for s in range(2):
        for g in range(2):
            blocks = [None] * 8
            for n in range(4):
                row = s * 4 + n
                base = base_buf[g, pl.ds(row, 8, stride=0), :]
                base = jnp.concatenate([base, base], axis=0).astype(BF16)
                home = (base - shift) + 128
                window = window_buf[g, row * 24 : row * 24 + 16, :].astype(BF16)
                for b in range(8):
                    piece = jnp.where(home == 128 + b, window, zero)
                    blocks[b] = piece if n == 0 else blocks[b] + piece
            for b in range(8):
                design_buf[g, s * 128 + b * 16 : s * 128 + b * 16 + 16, :] = blocks[b]


def force_rows(recv_ref, source, place, bufs):
    design_buf, force_buf = bufs[2:4]
    force_buf[...] = recv_ref[source, 12].astype(F32)
    first = lax.broadcasted_iota(jnp.int32, (16, 128), 0) == 0
    for g in range(2):
        row = force_buf[pl.ds(place * 2 + g, 8, stride=0), :]
        row = jnp.concatenate([row, row], axis=0)
        design_buf[g, 256:272, :] = jnp.where(first, row, 0.0).astype(BF16)


def build_tile(recv_ref, word, scale, bufs):
    source = (word >> 1) & 127
    place = word & 1
    spline_rows(recv_ref, source, place, scale, bufs)
    force_rows(recv_ref, source, place, bufs)
    build_design(bufs)


def products(bufs):
    design_buf = bufs[2]
    both = jnp.concatenate([design_buf[0], design_buf[1]], axis=1)
    return lax.dot_general(both, both[0:256], (((1,), (1,)), ((), ())), preferred_element_type=F32)


def sweep(count, word_at, recv_ref, add, bufs):
    bufs[2][...] = jnp.zeros_like(bufs[2])

    def step(i, carry):
        out = products(bufs)
        build_tile(recv_ref, word_at(i), 1.0 / 6.0, bufs)
        add(word_at(jnp.maximum(i - 1, 0)), out)
        return carry

    lax.fori_loop(0, count, step, 0)

    @pl.when(count > 0)
    def _():
        add(word_at(count - 1), products(bufs))


def edge_kernel(
    recv_ref, band_ref, rhs_ref, spill_ref, inner_list, bound_ref, meta_i32, first_mark, second_mark, edge_list,
    meta_sems, *bufs,
):
    devices = recv_ref.shape[0]
    totals = [jnp.zeros((8, 128), F32)] * 4
    for d in range(devices):
        totals[d % 4] = totals[d % 4] + recv_ref[d, 12].astype(F32)
    meta_i32[...] = (totals[0] + totals[1] + totals[2] + totals[3]).astype(jnp.int32)
    marks = (first_mark, second_mark)
    copies = [pltpu.make_async_copy(meta_i32.at[4 + q], marks[q], meta_sems.at[q]) for q in range(CAP)]
    for copy in copies:
        copy.start()
    band_ref[...] = jnp.zeros_like(band_ref)
    rhs_ref[...] = jnp.zeros_like(rhs_ref)
    spill_ref[...] = jnp.zeros_like(spill_ref)
    for copy in copies:
        copy.wait()

    def scan(d, counts):
        edges, others = counts
        for q in range(CAP):
            mark = marks[q][d]
            word = (mark << 8) + (d * CAP + q)
            at_edge = (mark == BLK_DEV).astype(jnp.int32)
            filled = jnp.minimum(mark, 1)
            edge_list[edges] = word
            inner_list[others] = word
            edges = edges + at_edge
            others = others + (filled - at_edge)
        return edges, others

    edges, others = lax.fori_loop(0, devices, scan, (0, 0), unroll=8)
    bound_ref[0] = others

    def add(word, out):
        band_ref[0] += out[0:128, 0:128]
        band_ref[1] += out[0:128, 128:256]
        spill_ref[0:128, :] += out[128:256, 128:256]
        rhs_ref[...] += out[256:264, 0:128]
        spill_ref[128:136, :] += out[256:264, 128:256]

    sweep(edges, lambda i: edge_list[i], recv_ref, add, bufs)


def inner_kernel(bound_ref, list_ref, recv_ref, edge_band_ref, edge_rhs_ref, band_ref, rhs_ref, *bufs):
    last = band_ref.shape[0] - 1
    band_ref[0:last] = jnp.zeros((last, 2, 128, 128), F32)
    band_ref[last] = edge_band_ref[...]
    rhs_ref[...] = jnp.zeros_like(rhs_ref)
    rhs_ref[last:last + 1] = edge_rhs_ref[0:1, :]

    def add(word, out):
        at = (word >> 8) - 1
        band_ref[at, 0] += out[0:128, 0:128]
        band_ref[at, 1] += out[0:128, 128:256]
        band_ref[at + 1, 0] += out[128:256, 128:256]
        rhs_ref[pl.ds(at, 1), :] += out[256:257, 0:128]
        rhs_ref[pl.ds(at + 1, 1), :] += out[256:257, 128:256]

    sweep(bound_ref[0], lambda i: list_ref[i], recv_ref, add, bufs)


def finish_kernel(band_ref, rhs_ref, spill_ref, band_hbm, rhs_hbm, first_band, first_rhs, sems):
    rest = pltpu.make_async_copy(band_ref.at[1:], band_hbm.at[1:], sems.at[0])
    lag = pltpu.make_async_copy(band_ref.at[0, 1], band_hbm.at[0, 1], sems.at[1])
    rest.start()
    lag.start()
    first_band[...] = band_ref[0, 0] + spill_ref[0:128, :]
    first_rhs[...] = rhs_ref[...]
    first_rhs[0:1, :] = rhs_ref[0:1, :] + spill_ref[128:129, :]
    diagonal = pltpu.make_async_copy(first_band, band_hbm.at[0, 0], sems.at[2])
    right = pltpu.make_async_copy(first_rhs, rhs_hbm, sems.at[3])
    diagonal.start()
    right.start()
    right.wait()
    diagonal.wait()
    lag.wait()
    rest.wait()


def buffers():
    return [
        pltpu.VMEM((2, 8, 128), F32),
        pltpu.VMEM((2, 192, 128), F32),
        pltpu.VMEM((2, 272, 128), BF16),
        pltpu.VMEM((8, 128), F32),
    ]


VMEM = pl.BlockSpec(memory_space=pltpu.VMEM)
SMEM = pl.BlockSpec(memory_space=pltpu.SMEM)
HBM = pl.BlockSpec(memory_space=pltpu.HBM)
SWEEP_COST = pl.CostEstimate(flops=4 << 30, bytes_accessed=4 << 20, transcendentals=0)


def edge(received):
    devices = received.shape[0]
    return pl.pallas_call(
        edge_kernel,
        out_shape=(
            jax.ShapeDtypeStruct((2, 128, 128), F32),
            jax.ShapeDtypeStruct((8, 128), F32),
            jax.ShapeDtypeStruct((136, 128), F32),
            jax.ShapeDtypeStruct((devices * CAP + 8,), jnp.int32),
            jax.ShapeDtypeStruct((1,), jnp.int32),
        ),
        in_specs=[VMEM],
        out_specs=(VMEM, VMEM, VMEM, SMEM, SMEM),
        scratch_shapes=[
            pltpu.VMEM((8, 128), jnp.int32),
            pltpu.SMEM((128,), jnp.int32),
            pltpu.SMEM((128,), jnp.int32),
            pltpu.SMEM((devices * CAP + 8,), jnp.int32),
            pltpu.SemaphoreType.DMA((CAP,)),
        ]
        + buffers(),
        compiler_params=pltpu.CompilerParams(vmem_limit_bytes=40 * MiB),
        cost_estimate=SWEEP_COST,
        name="edge",
    )(received)


def inner(bound, lists, received, edge_band, edge_rhs):
    return pl.pallas_call(
        inner_kernel,
        out_shape=(
            jax.ShapeDtypeStruct((BLK_DEV, 2, 128, 128), F32),
            jax.ShapeDtypeStruct((BLK_DEV, 128), F32),
        ),
        in_specs=[SMEM, SMEM, VMEM, VMEM, VMEM],
        out_specs=(VMEM, VMEM),
        scratch_shapes=buffers(),
        compiler_params=pltpu.CompilerParams(vmem_limit_bytes=40 * MiB),
        cost_estimate=SWEEP_COST,
        name="inner",
    )(bound, lists, received, edge_band, edge_rhs)


def finish(band, rhs, spill):
    return pl.pallas_call(
        finish_kernel,
        out_shape=(jax.ShapeDtypeStruct(band.shape, F32), jax.ShapeDtypeStruct(rhs.shape, F32)),
        in_specs=[VMEM, VMEM, VMEM],
        out_specs=(HBM, HBM),
        scratch_shapes=[
            pltpu.VMEM((128, 128), F32),
            pltpu.VMEM(rhs.shape, F32),
            pltpu.SemaphoreType.DMA((4,)),
        ],
        compiler_params=pltpu.CompilerParams(vmem_limit_bytes=16 * MiB),
        name="finish",
    )(band, rhs, spill)


def on_device(spline_index, spline_frac, projection, forces, row_owner, row_offset):
    device_count = lax.axis_size(AXES)
    me = lax.axis_index(AXES).astype(jnp.int32).reshape(1)
    sent = pack(row_owner[:, 0], row_offset, me, spline_index, spline_frac, projection, forces, device_count)
    received = lax.all_to_all(sent, AXES, split_axis=0, concat_axis=0, tiled=True)
    edge_band, edge_rhs, spill, lists, bound = edge(received)
    route = [(i, (i + 1) % device_count) for i in range(device_count)]
    spill = lax.ppermute(spill, AXES, route)
    band, rhs = inner(bound, lists, received, edge_band, edge_rhs)
    return finish(band, rhs, spill)


def solution(mesh):
    in_specs = (
        P(AXES, None, None, None),
        P(AXES, None, None, None),
        P(AXES, None, None, None),
        P(AXES, None),
        P(AXES, None),
        P(AXES),
    )
    out_specs = (P(AXES, None, None, None), P(AXES, None))
    return jax.shard_map(
        on_device, mesh=mesh, in_specs=in_specs, out_specs=out_specs, check_vma=False
    )
```

```python
import jax
import jax.numpy as jnp
from jax import lax
from jax.experimental import pallas as pl
from jax.experimental.pallas import tpu as pltpu
from jax.sharding import PartitionSpec as P

CO = 128
BLK_DEV = 22
CAP = 2
AXES = ("frame", "panel")
BF16 = jnp.bfloat16
F32 = jnp.float32
CHUNKS = 8
GROUP = 4
MiB = 1 << 20


def pack_kernel(
    owner_ref, offset_ref, me_ref, index_hbm, frac_hbm, proj_hbm, force_hbm, out_hbm,
    count_ref, index_ref, frac_ref, proj_ref, force_ref, force_f32, tile_ref, tail_f32, tail_ref,
    in_sems, force_sem, out_sem, tail_sem,
):
    device_count = out_hbm.shape[0]
    tiles = owner_ref.shape[0]
    step = tiles // CHUNKS
    arrays = ((index_hbm, index_ref), (frac_hbm, frac_ref), (proj_hbm, proj_ref))

    def fetch(a, c):
        part = pl.ds(c * step, step)
        return pltpu.make_async_copy(arrays[a][0].at[part], arrays[a][1].at[part], in_sems.at[a, c])

    force_copy = pltpu.make_async_copy(force_hbm, force_ref, force_sem)
    force_copy.start()
    for c in range(CHUNKS):
        for a in range(3):
            fetch(a, c).start()

    @pl.loop(0, device_count, unroll=8)
    def _(d):
        count_ref[d] = 0

    tail_f32[...] = jnp.zeros_like(tail_f32)
    here = lax.broadcasted_iota(jnp.int32, (1, 128), 1) == me_ref[0]
    force_copy.wait()
    force_f32[...] = force_ref[...].astype(F32)

    for c in range(CHUNKS):
        for a in range(3):
            fetch(a, c).wait()

        @pl.loop(c * step, (c + 1) * step, unroll=2)
        def _(t):
            owner = owner_ref[t]
            place = count_ref[owner]
            count_ref[owner] = place + 1
            for a in range(3):
                ref = arrays[a][1]
                for g in range(2):
                    low = ref[t, 0, :, g * 128 : g * 128 + 128].astype(F32)
                    high = ref[t, 1, :, g * 128 : g * 128 + 128].astype(F32)
                    tile_ref[t, a * 2 + g] = jnp.concatenate([low, high], axis=0).astype(BF16)
            pltpu.make_async_copy(tile_ref.at[t], out_hbm.at[owner, pl.ds(place * 6, 6)], out_sem).start()
            row = force_f32[pl.ds(t, 1), :]
            for g in range(2):
                tail_f32[owner, pl.ds(place * 2 + g, 1), :] = row[:, g * 128 : g * 128 + 128]
            tail_f32[owner, pl.ds(4 + place, 1), :] = jnp.where(here, (offset_ref[t] + 1).astype(F32), 0.0)

    tail_ref[...] = tail_f32[...].astype(BF16)
    tail_copy = pltpu.make_async_copy(tail_ref, out_hbm.at[:, 12], tail_sem)
    tail_copy.start()
    tail_copy.wait()
    pltpu.make_async_copy(tile_ref, tile_ref, out_sem).wait()


def pack(owners, offsets, me, spline_index, spline_frac, projection, forces, device_count):
    hbm = pl.BlockSpec(memory_space=pltpu.HBM)
    smem = pl.BlockSpec(memory_space=pltpu.SMEM)
    tiles = owners.shape[0]
    return pl.pallas_call(
        pack_kernel,
        out_shape=jax.ShapeDtypeStruct((device_count, 13, 8, 128), BF16),
        in_specs=[smem, smem, smem, hbm, hbm, hbm, hbm],
        out_specs=hbm,
        scratch_shapes=[
            pltpu.SMEM((device_count,), jnp.int32),
            pltpu.VMEM(spline_index.shape, spline_index.dtype),
            pltpu.VMEM(spline_frac.shape, BF16),
            pltpu.VMEM(projection.shape, BF16),
            pltpu.VMEM(forces.shape, BF16),
            pltpu.VMEM(forces.shape, F32),
            pltpu.VMEM((tiles, 6, 8, 128), BF16),
            pltpu.VMEM((device_count, 8, 128), F32),
            pltpu.VMEM((device_count, 8, 128), BF16),
            pltpu.SemaphoreType.DMA((3, CHUNKS)),
            pltpu.SemaphoreType.DMA,
            pltpu.SemaphoreType.DMA,
            pltpu.SemaphoreType.DMA,
        ],
        compiler_params=pltpu.CompilerParams(vmem_limit_bytes=60 * MiB),
        name="pack",
    )(owners, offsets, me, spline_index, spline_frac, projection, forces)


def spline_rows(recv_ref, source, place, scale, bufs):
    base_buf, window_buf = bufs[0:2]
    pieces = [[], [], [], []]
    lows = []
    for g in range(2):
        index = recv_ref[source, place * 6 + g].astype(F32)
        t = recv_ref[source, place * 6 + 2 + g].astype(F32)
        q = recv_ref[source, place * 6 + 4 + g].astype(F32) * scale
        base_buf[g] = index * (1.0 / 16.0)
        lows.append((index.astype(jnp.int32) & 15).astype(F32))
        u = 1.0 - t
        t2 = t * t
        t3 = t2 * t
        pieces[0].append(q * (u * u * u))
        pieces[1].append(q * (3.0 * t3 - 6.0 * t2 + 4.0))
        pieces[2].append(q * (3.0 * (t + t2 - t3) + 1.0))
        pieces[3].append(q * t3)
    low = jnp.concatenate(lows, axis=0).astype(BF16)
    pieces = [jnp.concatenate(p, axis=0).astype(BF16) for p in pieces]
    starts = [low == k for k in range(16)]
    zero = jnp.zeros((16, 128), BF16)
    for k in range(16):
        value = zero
        for m in range(4):
            value = jnp.where(starts[(k - m) % 16], pieces[m], value)
        value = value.astype(F32)
        for g in range(2):
            window_buf[g, pl.ds(k, 8, stride=24), :] = value[g * 8 : g * 8 + 8]


def build_design(bufs):
    base_buf, window_buf, design_buf = bufs[0:3]
    shift = (lax.broadcasted_iota(jnp.int32, (16, 128), 0).astype(F32) * (1.0 / 16.0) - 7.5 / 16.0).astype(BF16)
    zero = jnp.zeros((16, 128), BF16)
    for s in range(2):
        for g in range(2):
            blocks = [None] * 8
            for n in range(4):
                row = s * 4 + n
                base = base_buf[g, pl.ds(row, 8, stride=0), :]
                base = jnp.concatenate([base, base], axis=0).astype(BF16)
                home = (base - shift) + 128
                window = window_buf[g, row * 24 : row * 24 + 16, :].astype(BF16)
                for b in range(8):
                    piece = jnp.where(home == 128 + b, window, zero)
                    blocks[b] = piece if n == 0 else blocks[b] + piece
            for b in range(8):
                design_buf[g, s * 128 + b * 16 : s * 128 + b * 16 + 16, :] = blocks[b]


def force_rows(recv_ref, source, place, bufs):
    design_buf, force_buf = bufs[2:4]
    force_buf[...] = recv_ref[source, 12].astype(F32)
    first = lax.broadcasted_iota(jnp.int32, (16, 128), 0) == 0
    for g in range(2):
        row = force_buf[pl.ds(place * 2 + g, 8, stride=0), :]
        row = jnp.concatenate([row, row], axis=0)
        design_buf[g, 256:272, :] = jnp.where(first, row, 0.0).astype(BF16)


def build_tile(recv_ref, word, scale, bufs):
    source = (word >> 1) & 127
    place = word & 1
    spline_rows(recv_ref, source, place, scale, bufs)
    force_rows(recv_ref, source, place, bufs)
    build_design(bufs)


def products(bufs):
    design_buf = bufs[2]
    both = jnp.concatenate([design_buf[0], design_buf[1]], axis=1)
    return lax.dot_general(both, both[0:256], (((1,), (1,)), ((), ())), preferred_element_type=F32)


def sweep(count, word_at, recv_ref, add, bufs):
    sets = [bufs[u * 4 : u * 4 + 4] for u in range(GROUP)]
    for group in sets:
        group[2][...] = jnp.zeros_like(group[2])

    def clamped(i):
        return word_at(jnp.clip(i, 0, count - 1))

    def step(j, carry):
        first = j * GROUP
        for u in range(GROUP):
            out = products(sets[u])
            i = first + u
            scale = jnp.where(i < count, 1.0 / 6.0, 0.0).astype(F32)
            build_tile(recv_ref, clamped(i), scale, sets[u])
            add(clamped(i - GROUP), out)
        return carry

    turns = (count + GROUP - 1) // GROUP
    lax.fori_loop(0, turns, step, 0)

    @pl.when(count > 0)
    def _():
        for u in range(GROUP):
            add(clamped((turns - 1) * GROUP + u), products(sets[u]))


def edge_kernel(
    recv_ref, band_ref, rhs_ref, spill_ref, inner_list, bound_ref, meta_i32, first_mark, second_mark, edge_list,
    meta_sems, *bufs,
):
    devices = recv_ref.shape[0]
    totals = [jnp.zeros((8, 128), F32)] * 4
    for d in range(devices):
        totals[d % 4] = totals[d % 4] + recv_ref[d, 12].astype(F32)
    meta_i32[...] = (totals[0] + totals[1] + totals[2] + totals[3]).astype(jnp.int32)
    marks = (first_mark, second_mark)
    copies = [pltpu.make_async_copy(meta_i32.at[4 + q], marks[q], meta_sems.at[q]) for q in range(CAP)]
    for copy in copies:
        copy.start()
    band_ref[...] = jnp.zeros_like(band_ref)
    rhs_ref[...] = jnp.zeros_like(rhs_ref)
    spill_ref[...] = jnp.zeros_like(spill_ref)
    for copy in copies:
        copy.wait()

    def scan(d, counts):
        edges, others = counts
        for q in range(CAP):
            mark = marks[q][d]
            word = (mark << 8) + (d * CAP + q)
            at_edge = (mark == BLK_DEV).astype(jnp.int32)
            filled = jnp.minimum(mark, 1)
            edge_list[edges] = word
            inner_list[others] = word
            edges = edges + at_edge
            others = others + (filled - at_edge)
        return edges, others

    edges, others = lax.fori_loop(0, devices, scan, (0, 0), unroll=8)
    bound_ref[0] = others

    def add(word, out):
        band_ref[0] += out[0:128, 0:128]
        band_ref[1] += out[0:128, 128:256]
        spill_ref[0:128, :] += out[128:256, 128:256]
        rhs_ref[...] += out[256:264, 0:128]
        spill_ref[128:136, :] += out[256:264, 128:256]

    sweep(edges, lambda i: edge_list[i], recv_ref, add, bufs)


def inner_kernel(bound_ref, list_ref, recv_ref, edge_band_ref, edge_rhs_ref, band_ref, rhs_ref, *bufs):
    last = band_ref.shape[0] - 1
    band_ref[0:last] = jnp.zeros((last, 2, 128, 128), F32)
    band_ref[last] = edge_band_ref[...]
    rhs_ref[...] = jnp.zeros_like(rhs_ref)
    rhs_ref[last:last + 1] = edge_rhs_ref[0:1, :]

    def add(word, out):
        at = (word >> 8) - 1
        band_ref[at, 0] += out[0:128, 0:128]
        band_ref[at, 1] += out[0:128, 128:256]
        band_ref[at + 1, 0] += out[128:256, 128:256]
        rhs_ref[pl.ds(at, 1), :] += out[256:257, 0:128]
        rhs_ref[pl.ds(at + 1, 1), :] += out[256:257, 128:256]

    sweep(bound_ref[0], lambda i: list_ref[i], recv_ref, add, bufs)


def finish_kernel(band_ref, rhs_ref, spill_ref, band_hbm, rhs_hbm, first_band, first_rhs, sems):
    rest = pltpu.make_async_copy(band_ref.at[1:], band_hbm.at[1:], sems.at[0])
    lag = pltpu.make_async_copy(band_ref.at[0, 1], band_hbm.at[0, 1], sems.at[1])
    rest.start()
    lag.start()
    first_band[...] = band_ref[0, 0] + spill_ref[0:128, :]
    first_rhs[...] = rhs_ref[...]
    first_rhs[0:1, :] = rhs_ref[0:1, :] + spill_ref[128:129, :]
    diagonal = pltpu.make_async_copy(first_band, band_hbm.at[0, 0], sems.at[2])
    right = pltpu.make_async_copy(first_rhs, rhs_hbm, sems.at[3])
    diagonal.start()
    right.start()
    right.wait()
    diagonal.wait()
    lag.wait()
    rest.wait()


def buffers():
    return [
        pltpu.VMEM((2, 8, 128), F32),
        pltpu.VMEM((2, 192, 128), F32),
        pltpu.VMEM((2, 272, 128), BF16),
        pltpu.VMEM((8, 128), F32),
    ] * GROUP


VMEM = pl.BlockSpec(memory_space=pltpu.VMEM)
SMEM = pl.BlockSpec(memory_space=pltpu.SMEM)
HBM = pl.BlockSpec(memory_space=pltpu.HBM)
SWEEP_COST = pl.CostEstimate(flops=4 << 30, bytes_accessed=4 << 20, transcendentals=0)


def edge(received):
    devices = received.shape[0]
    return pl.pallas_call(
        edge_kernel,
        out_shape=(
            jax.ShapeDtypeStruct((2, 128, 128), F32),
            jax.ShapeDtypeStruct((8, 128), F32),
            jax.ShapeDtypeStruct((136, 128), F32),
            jax.ShapeDtypeStruct((devices * CAP + 8,), jnp.int32),
            jax.ShapeDtypeStruct((1,), jnp.int32),
        ),
        in_specs=[VMEM],
        out_specs=(VMEM, VMEM, VMEM, SMEM, SMEM),
        scratch_shapes=[
            pltpu.VMEM((8, 128), jnp.int32),
            pltpu.SMEM((128,), jnp.int32),
            pltpu.SMEM((128,), jnp.int32),
            pltpu.SMEM((devices * CAP + 8,), jnp.int32),
            pltpu.SemaphoreType.DMA((CAP,)),
        ]
        + buffers(),
        compiler_params=pltpu.CompilerParams(vmem_limit_bytes=40 * MiB),
        cost_estimate=SWEEP_COST,
        name="edge",
    )(received)


def inner(bound, lists, received, edge_band, edge_rhs):
    return pl.pallas_call(
        inner_kernel,
        out_shape=(
            jax.ShapeDtypeStruct((BLK_DEV, 2, 128, 128), F32),
            jax.ShapeDtypeStruct((BLK_DEV, 128), F32),
        ),
        in_specs=[SMEM, SMEM, VMEM, VMEM, VMEM],
        out_specs=(VMEM, VMEM),
        scratch_shapes=buffers(),
        compiler_params=pltpu.CompilerParams(vmem_limit_bytes=40 * MiB),
        cost_estimate=SWEEP_COST,
        name="inner",
    )(bound, lists, received, edge_band, edge_rhs)


def finish(band, rhs, spill):
    return pl.pallas_call(
        finish_kernel,
        out_shape=(jax.ShapeDtypeStruct(band.shape, F32), jax.ShapeDtypeStruct(rhs.shape, F32)),
        in_specs=[VMEM, VMEM, VMEM],
        out_specs=(HBM, HBM),
        scratch_shapes=[
            pltpu.VMEM((128, 128), F32),
            pltpu.VMEM(rhs.shape, F32),
            pltpu.SemaphoreType.DMA((4,)),
        ],
        compiler_params=pltpu.CompilerParams(vmem_limit_bytes=16 * MiB),
        name="finish",
    )(band, rhs, spill)


def on_device(spline_index, spline_frac, projection, forces, row_owner, row_offset):
    device_count = lax.axis_size(AXES)
    me = lax.axis_index(AXES).astype(jnp.int32).reshape(1)
    sent = pack(row_owner[:, 0], row_offset, me, spline_index, spline_frac, projection, forces, device_count)
    received = lax.all_to_all(sent, AXES, split_axis=0, concat_axis=0, tiled=True)
    edge_band, edge_rhs, spill, lists, bound = edge(received)
    route = [(i, (i + 1) % device_count) for i in range(device_count)]
    spill = lax.ppermute(spill, AXES, route)
    band, rhs = inner(bound, lists, received, edge_band, edge_rhs)
    return finish(band, rhs, spill)


def solution(mesh):
    in_specs = (
        P(AXES, None, None, None),
        P(AXES, None, None, None),
        P(AXES, None, None, None),
        P(AXES, None),
        P(AXES, None),
        P(AXES),
    )
    out_specs = (P(AXES, None, None, None), P(AXES, None))
    return jax.shard_map(
        on_device, mesh=mesh, in_specs=in_specs, out_specs=out_specs, check_vma=False
    )
```

```python
import jax
import jax.numpy as jnp
from jax import lax
from jax.experimental import pallas as pl
from jax.experimental.pallas import tpu as pltpu
from jax.sharding import PartitionSpec as P

CO = 128
BLK_DEV = 22
CAP = 2
AXES = ("frame", "panel")
BF16 = jnp.bfloat16
F32 = jnp.float32
CHUNKS = 8
GROUP = 8
MiB = 1 << 20


def pack_kernel(
    owner_ref, offset_ref, me_ref, index_hbm, frac_hbm, proj_hbm, force_hbm, out_hbm,
    count_ref, index_ref, frac_ref, proj_ref, force_ref, force_f32, tile_ref, tail_f32, tail_ref,
    in_sems, force_sem, out_sem, tail_sem,
):
    device_count = out_hbm.shape[0]
    tiles = owner_ref.shape[0]
    step = tiles // CHUNKS
    arrays = ((index_hbm, index_ref), (frac_hbm, frac_ref), (proj_hbm, proj_ref))

    def fetch(a, c):
        part = pl.ds(c * step, step)
        return pltpu.make_async_copy(arrays[a][0].at[part], arrays[a][1].at[part], in_sems.at[a, c])

    force_copy = pltpu.make_async_copy(force_hbm, force_ref, force_sem)
    force_copy.start()
    for c in range(CHUNKS):
        for a in range(3):
            fetch(a, c).start()

    @pl.loop(0, device_count, unroll=8)
    def _(d):
        count_ref[d] = 0

    tail_f32[...] = jnp.zeros_like(tail_f32)
    here = lax.broadcasted_iota(jnp.int32, (1, 128), 1) == me_ref[0]
    force_copy.wait()
    force_f32[...] = force_ref[...].astype(F32)

    for c in range(CHUNKS):
        for a in range(3):
            fetch(a, c).wait()

        @pl.loop(c * step, (c + 1) * step, unroll=2)
        def _(t):
            owner = owner_ref[t]
            place = count_ref[owner]
            count_ref[owner] = place + 1
            for a in range(3):
                ref = arrays[a][1]
                for g in range(2):
                    low = ref[t, 0, :, g * 128 : g * 128 + 128].astype(F32)
                    high = ref[t, 1, :, g * 128 : g * 128 + 128].astype(F32)
                    tile_ref[t, a * 2 + g] = jnp.concatenate([low, high], axis=0).astype(BF16)
            pltpu.make_async_copy(tile_ref.at[t], out_hbm.at[owner, pl.ds(place * 6, 6)], out_sem).start()
            row = force_f32[pl.ds(t, 1), :]
            for g in range(2):
                tail_f32[owner, pl.ds(place * 2 + g, 1), :] = row[:, g * 128 : g * 128 + 128]
            tail_f32[owner, pl.ds(4 + place, 1), :] = jnp.where(here, (offset_ref[t] + 1).astype(F32), 0.0)

    tail_ref[...] = tail_f32[...].astype(BF16)
    tail_copy = pltpu.make_async_copy(tail_ref, out_hbm.at[:, 12], tail_sem)
    tail_copy.start()
    tail_copy.wait()
    pltpu.make_async_copy(tile_ref, tile_ref, out_sem).wait()


def pack(owners, offsets, me, spline_index, spline_frac, projection, forces, device_count):
    hbm = pl.BlockSpec(memory_space=pltpu.HBM)
    smem = pl.BlockSpec(memory_space=pltpu.SMEM)
    tiles = owners.shape[0]
    return pl.pallas_call(
        pack_kernel,
        out_shape=jax.ShapeDtypeStruct((device_count, 13, 8, 128), BF16),
        in_specs=[smem, smem, smem, hbm, hbm, hbm, hbm],
        out_specs=hbm,
        scratch_shapes=[
            pltpu.SMEM((device_count,), jnp.int32),
            pltpu.VMEM(spline_index.shape, spline_index.dtype),
            pltpu.VMEM(spline_frac.shape, BF16),
            pltpu.VMEM(projection.shape, BF16),
            pltpu.VMEM(forces.shape, BF16),
            pltpu.VMEM(forces.shape, F32),
            pltpu.VMEM((tiles, 6, 8, 128), BF16),
            pltpu.VMEM((device_count, 8, 128), F32),
            pltpu.VMEM((device_count, 8, 128), BF16),
            pltpu.SemaphoreType.DMA((3, CHUNKS)),
            pltpu.SemaphoreType.DMA,
            pltpu.SemaphoreType.DMA,
            pltpu.SemaphoreType.DMA,
        ],
        compiler_params=pltpu.CompilerParams(vmem_limit_bytes=60 * MiB),
        name="pack",
    )(owners, offsets, me, spline_index, spline_frac, projection, forces)


def spline_rows(recv_ref, source, place, scale, bufs):
    base_buf, window_buf = bufs[0:2]
    pieces = [[], [], [], []]
    lows = []
    for g in range(2):
        index = recv_ref[source, place * 6 + g].astype(F32)
        t = recv_ref[source, place * 6 + 2 + g].astype(F32)
        q = recv_ref[source, place * 6 + 4 + g].astype(F32) * scale
        base_buf[g] = index * (1.0 / 8.0)
        lows.append((index.astype(jnp.int32) & 7).astype(F32))
        u = 1.0 - t
        t2 = t * t
        t3 = t2 * t
        pieces[0].append(q * (u * u * u))
        pieces[1].append(q * (3.0 * t3 - 6.0 * t2 + 4.0))
        pieces[2].append(q * (3.0 * (t + t2 - t3) + 1.0))
        pieces[3].append(q * t3)
    low = jnp.concatenate(lows, axis=0).astype(BF16)
    pieces = [jnp.concatenate(p, axis=0).astype(BF16) for p in pieces]
    starts = [low == k for k in range(8)]
    zero = jnp.zeros((16, 128), BF16)
    for k in range(8):
        value = zero
        for m in range(4):
            value = jnp.where(starts[(k - m) % 8], pieces[m], value)
        value = value.astype(F32)
        for g in range(2):
            window_buf[g, pl.ds(k, 8, stride=8), :] = value[g * 8 : g * 8 + 8]


def build_design(bufs):
    base_buf, window_buf, design_buf = bufs[0:3]
    k = (lax.broadcasted_iota(jnp.int32, (16, 128), 0) & 7).astype(F32)
    shift = (k * (1.0 / 8.0) - 7.0 / 16.0).astype(BF16)
    zero = jnp.zeros((16, 128), BF16)
    for s in range(2):
        blocks = [None] * 16
        for n in range(4):
            row = s * 4 + n
            base = [base_buf[g, pl.ds(row, 8, stride=0), :] for g in range(2)]
            base = jnp.concatenate(base, axis=0).astype(BF16)
            home = (base - shift) + 128
            window = [window_buf[g, row * 8 : row * 8 + 8, :] for g in range(2)]
            window = jnp.concatenate(window, axis=0).astype(BF16)
            for b in range(16):
                piece = jnp.where(home == 128 + b, window, zero)
                blocks[b] = piece if n == 0 else blocks[b] + piece
        for b in range(16):
            at = s * 128 + b * 8
            design_buf[at : at + 8, 0:128] = blocks[b][0:8]
            design_buf[at : at + 8, 128:256] = blocks[b][8:16]


def force_rows(recv_ref, source, place, bufs):
    design_buf, force_buf = bufs[2:4]
    force_buf[...] = recv_ref[source, 12].astype(F32)
    first = lax.broadcasted_iota(jnp.int32, (16, 128), 0) == 0
    rows = []
    for g in range(2):
        row = force_buf[pl.ds(place * 2 + g, 8, stride=0), :]
        row = jnp.concatenate([row, row], axis=0)
        rows.append(jnp.where(first, row, 0.0).astype(BF16))
    design_buf[256:272, :] = jnp.concatenate(rows, axis=1)


def build_tile(recv_ref, word, scale, bufs):
    source = (word >> 1) & 127
    place = word & 1
    spline_rows(recv_ref, source, place, scale, bufs)
    force_rows(recv_ref, source, place, bufs)
    build_design(bufs)


def products(bufs):
    design_buf = bufs[2]
    return lax.dot_general(
        design_buf[...], design_buf[0:256, :], (((1,), (1,)), ((), ())), preferred_element_type=F32
    )


def sweep(count, word_at, recv_ref, add, bufs):
    sets = [bufs[u * 4 : u * 4 + 4] for u in range(GROUP)]
    for group in sets:
        group[2][...] = jnp.zeros_like(group[2])

    def clamped(i):
        return word_at(jnp.clip(i, 0, count - 1))

    def step(j, carry):
        first = j * GROUP
        for u in range(GROUP):
            out = products(sets[u])
            i = first + u
            scale = jnp.where(i < count, 1.0 / 6.0, 0.0).astype(F32)
            build_tile(recv_ref, clamped(i), scale, sets[u])
            add(clamped(i - GROUP), out)
        return carry

    turns = (count + GROUP - 1) // GROUP
    lax.fori_loop(0, turns, step, 0)

    @pl.when(count > 0)
    def _():
        for u in range(GROUP):
            add(clamped((turns - 1) * GROUP + u), products(sets[u]))


def edge_kernel(
    recv_ref, band_ref, rhs_ref, spill_ref, list_ref, bound_ref, meta_i32, first_words, second_words, edge_count,
    other_count, meta_sems, *bufs,
):
    counts = (edge_count, other_count)
    devices = recv_ref.shape[0]
    totals = [jnp.zeros((8, 128), F32)] * 4
    for d in range(devices):
        totals[d % 4] = totals[d % 4] + recv_ref[d, 12].astype(F32)
    mark = (totals[0] + totals[1] + totals[2] + totals[3])[4 : 4 + CAP]
    at_edge = mark == BLK_DEV
    other = (mark > 0) & (mark < BLK_DEV)
    kinds = jnp.concatenate([at_edge.astype(F32), other.astype(F32), jnp.zeros((4, 128), F32)], axis=0)
    ahead = lax.broadcasted_iota(jnp.int32, (128, 128), 0) < lax.broadcasted_iota(jnp.int32, (128, 128), 1)
    rank = lax.dot_general(
        kinds.astype(BF16), ahead.astype(F32).astype(BF16), (((1,), (0,)), ((), ())), preferred_element_type=F32
    )
    sums = jnp.sum(kinds, axis=1, keepdims=True)
    rank_edge = jnp.concatenate([rank[0:1], rank[1:2] + sums[0:1]], axis=0)
    rank_other = jnp.concatenate([rank[2:3], rank[3:4] + sums[2:3]], axis=0)
    slots = devices * CAP
    where_to = jnp.where(at_edge, rank_edge, jnp.where(other, slots - 1 - rank_other, slots)).astype(jnp.int32)
    shape = (CAP, 128)
    code = lax.broadcasted_iota(jnp.int32, shape, 1) * CAP + lax.broadcasted_iota(jnp.int32, shape, 0)
    meta_i32[0:CAP] = where_to * 65536 + mark.astype(jnp.int32) * 256 + code
    meta_i32[2:3] = jnp.broadcast_to(sums[0:1] + sums[1:2], (1, 128)).astype(jnp.int32)
    meta_i32[3:4] = jnp.broadcast_to(sums[2:3] + sums[3:4], (1, 128)).astype(jnp.int32)
    words = (first_words, second_words)
    copies = [pltpu.make_async_copy(meta_i32.at[k], ref, meta_sems.at[k]) for k, ref in enumerate(words + tuple(counts))]
    for copy in copies:
        copy.start()
    band_ref[...] = jnp.zeros_like(band_ref)
    rhs_ref[...] = jnp.zeros_like(rhs_ref)
    spill_ref[...] = jnp.zeros_like(spill_ref)
    for copy in copies:
        copy.wait()

    @pl.loop(0, devices, unroll=8)
    def _(d):
        for q in range(CAP):
            word = words[q][d]
            list_ref[word >> 16] = word

    bound_ref[0] = counts[1][0]

    def add(word, out):
        band_ref[0] += out[0:128, 0:128]
        band_ref[1] += out[0:128, 128:256]
        spill_ref[0:128, :] += out[128:256, 128:256]
        rhs_ref[...] += out[256:264, 0:128]
        spill_ref[128:136, :] += out[256:264, 128:256]

    sweep(counts[0][0], lambda i: list_ref[i], recv_ref, add, bufs)


def inner_kernel(bound_ref, list_ref, recv_ref, edge_band_ref, edge_rhs_ref, band_ref, rhs_ref, *bufs):
    last = band_ref.shape[0] - 1
    band_ref[0:last] = jnp.zeros((last, 2, 128, 128), F32)
    band_ref[last] = edge_band_ref[...]
    rhs_ref[...] = jnp.zeros_like(rhs_ref)
    rhs_ref[last:last + 1] = edge_rhs_ref[0:1, :]

    def add(word, out):
        at = ((word >> 8) & 255) - 1
        band_ref[at, 0] += out[0:128, 0:128]
        band_ref[at, 1] += out[0:128, 128:256]
        band_ref[at + 1, 0] += out[128:256, 128:256]
        rhs_ref[pl.ds(at, 1), :] += out[256:257, 0:128]
        rhs_ref[pl.ds(at + 1, 1), :] += out[256:257, 128:256]

    sweep(bound_ref[0], lambda i: list_ref[recv_ref.shape[0] * CAP - 1 - i], recv_ref, add, bufs)


def finish_kernel(band_ref, rhs_ref, spill_ref, band_hbm, rhs_hbm, first_band, first_rhs, sems):
    rest = pltpu.make_async_copy(band_ref.at[1:], band_hbm.at[1:], sems.at[0])
    lag = pltpu.make_async_copy(band_ref.at[0, 1], band_hbm.at[0, 1], sems.at[1])
    rest.start()
    lag.start()
    first_band[...] = band_ref[0, 0] + spill_ref[0:128, :]
    first_rhs[...] = rhs_ref[...]
    first_rhs[0:1, :] = rhs_ref[0:1, :] + spill_ref[128:129, :]
    diagonal = pltpu.make_async_copy(first_band, band_hbm.at[0, 0], sems.at[2])
    right = pltpu.make_async_copy(first_rhs, rhs_hbm, sems.at[3])
    diagonal.start()
    right.start()
    right.wait()
    diagonal.wait()
    lag.wait()
    rest.wait()


def buffers():
    return [
        pltpu.VMEM((2, 8, 128), F32),
        pltpu.VMEM((2, 64, 128), F32),
        pltpu.VMEM((272, 256), BF16),
        pltpu.VMEM((8, 128), F32),
    ] * GROUP


VMEM = pl.BlockSpec(memory_space=pltpu.VMEM)
SMEM = pl.BlockSpec(memory_space=pltpu.SMEM)
HBM = pl.BlockSpec(memory_space=pltpu.HBM)
SWEEP_COST = pl.CostEstimate(flops=4 << 30, bytes_accessed=4 << 20, transcendentals=0)


def edge(received):
    devices = received.shape[0]
    return pl.pallas_call(
        edge_kernel,
        out_shape=(
            jax.ShapeDtypeStruct((2, 128, 128), F32),
            jax.ShapeDtypeStruct((8, 128), F32),
            jax.ShapeDtypeStruct((136, 128), F32),
            jax.ShapeDtypeStruct((devices * CAP + 8,), jnp.int32),
            jax.ShapeDtypeStruct((1,), jnp.int32),
        ),
        in_specs=[VMEM],
        out_specs=(VMEM, VMEM, VMEM, SMEM, SMEM),
        scratch_shapes=[
            pltpu.VMEM((8, 128), jnp.int32),
            pltpu.SMEM((128,), jnp.int32),
            pltpu.SMEM((128,), jnp.int32),
            pltpu.SMEM((128,), jnp.int32),
            pltpu.SMEM((128,), jnp.int32),
            pltpu.SemaphoreType.DMA((4,)),
        ]
        + buffers(),
        compiler_params=pltpu.CompilerParams(vmem_limit_bytes=40 * MiB),
        cost_estimate=SWEEP_COST,
        name="edge",
    )(received)


def inner(bound, lists, received, edge_band, edge_rhs):
    return pl.pallas_call(
        inner_kernel,
        out_shape=(
            jax.ShapeDtypeStruct((BLK_DEV, 2, 128, 128), F32),
            jax.ShapeDtypeStruct((BLK_DEV, 128), F32),
        ),
        in_specs=[SMEM, SMEM, VMEM, VMEM, VMEM],
        out_specs=(VMEM, VMEM),
        scratch_shapes=buffers(),
        compiler_params=pltpu.CompilerParams(vmem_limit_bytes=40 * MiB),
        cost_estimate=SWEEP_COST,
        name="inner",
    )(bound, lists, received, edge_band, edge_rhs)


def finish(band, rhs, spill):
    return pl.pallas_call(
        finish_kernel,
        out_shape=(jax.ShapeDtypeStruct(band.shape, F32), jax.ShapeDtypeStruct(rhs.shape, F32)),
        in_specs=[VMEM, VMEM, VMEM],
        out_specs=(HBM, HBM),
        scratch_shapes=[
            pltpu.VMEM((128, 128), F32),
            pltpu.VMEM(rhs.shape, F32),
            pltpu.SemaphoreType.DMA((4,)),
        ],
        compiler_params=pltpu.CompilerParams(vmem_limit_bytes=16 * MiB),
        name="finish",
    )(band, rhs, spill)


def on_device(spline_index, spline_frac, projection, forces, row_owner, row_offset):
    device_count = lax.axis_size(AXES)
    me = lax.axis_index(AXES).astype(jnp.int32).reshape(1)
    sent = pack(row_owner[:, 0], row_offset, me, spline_index, spline_frac, projection, forces, device_count)
    received = lax.all_to_all(sent, AXES, split_axis=0, concat_axis=0, tiled=True)
    edge_band, edge_rhs, spill, lists, bound = edge(received)
    route = [(i, (i + 1) % device_count) for i in range(device_count)]
    spill = lax.ppermute(spill, AXES, route)
    band, rhs = inner(bound, lists, received, edge_band, edge_rhs)
    return finish(band, rhs, spill)


def solution(mesh):
    in_specs = (
        P(AXES, None, None, None),
        P(AXES, None, None, None),
        P(AXES, None, None, None),
        P(AXES, None),
        P(AXES, None),
        P(AXES),
    )
    out_specs = (P(AXES, None, None, None), P(AXES, None))
    return jax.shard_map(
        on_device, mesh=mesh, in_specs=in_specs, out_specs=out_specs, check_vma=False
    )
```

```python
import jax
import jax.numpy as jnp
from jax import lax
from jax.experimental import pallas as pl
from jax.experimental.pallas import tpu as pltpu
from jax.sharding import PartitionSpec as P

CO = 128
BLK_DEV = 22
CAP = 2
AXES = ("frame", "panel")
BF16 = jnp.bfloat16
F32 = jnp.float32
CHUNKS = 2
GROUP = 8
MiB = 1 << 20


def pack_kernel(
    owner_hbm, offset_hbm, index_hbm, frac_hbm, proj_hbm, force_hbm, out_hbm,
    owner_ref, offset_ref, count_ref, slot_ref, index_ref, frac_ref, proj_ref, force_ref, force_f32, tile_ref, tail_f32, tail_ref,
    in_sems, force_sem, out_sem, tail_sem, row_sems,
):
    device_count = out_hbm.shape[0]
    tiles = owner_ref.shape[0]
    step = tiles // CHUNKS
    arrays = ((index_hbm, index_ref), (frac_hbm, frac_ref), (proj_hbm, proj_ref))

    def fetch(a, c):
        part = pl.ds(c * step, step)
        return pltpu.make_async_copy(arrays[a][0].at[part], arrays[a][1].at[part], in_sems.at[a, c])

    force_copy = pltpu.make_async_copy(force_hbm, force_ref, force_sem)
    owner_copy = pltpu.make_async_copy(owner_hbm, owner_ref, row_sems.at[0])
    offset_copy = pltpu.make_async_copy(offset_hbm, offset_ref, row_sems.at[1])
    force_copy.start()
    owner_copy.start()
    offset_copy.start()
    for c in range(CHUNKS):
        for a in range(3):
            fetch(a, c).start()

    @pl.loop(0, device_count, unroll=8)
    def _(d):
        count_ref[d] = 0

    tail_f32[...] = jnp.zeros_like(tail_f32)
    me = lax.axis_index(AXES[0]) * lax.axis_size(AXES[1]) + lax.axis_index(AXES[1])
    here = lax.broadcasted_iota(jnp.int32, (1, 128), 1) == me
    owner_copy.wait()
    offset_copy.wait()
    force_copy.wait()
    force_f32[...] = force_ref[...].astype(F32)

    @pl.loop(0, tiles, unroll=4)
    def _(t):
        owner = owner_ref[t]
        place = count_ref[owner]
        count_ref[owner] = place + 1
        slot_ref[t] = owner * CAP + place
        row = force_f32[pl.ds(t, 1), :]
        for g in range(2):
            tail_f32[owner, pl.ds(place * 2 + g, 1), :] = row[:, g * 128 : g * 128 + 128]
        tail_f32[owner, pl.ds(4 + place, 1), :] = jnp.where(here, (offset_ref[t] + 1).astype(F32), 0.0)

    tail_ref[...] = tail_f32[...].astype(BF16)
    tail_copy = pltpu.make_async_copy(tail_ref, out_hbm.at[:, 12], tail_sem)
    tail_copy.start()

    for c in range(CHUNKS):
        for a in range(3):
            fetch(a, c).wait()

        @pl.loop(c * step, (c + 1) * step, unroll=4)
        def _(t):
            slot = slot_ref[t]
            for a in range(3):
                ref = arrays[a][1]
                for g in range(2):
                    low = ref[t, 0, :, g * 128 : g * 128 + 128].astype(F32)
                    high = ref[t, 1, :, g * 128 : g * 128 + 128].astype(F32)
                    tile_ref[t, a * 2 + g] = jnp.concatenate([low, high], axis=0).astype(BF16)
            target = out_hbm.at[slot >> 1, pl.ds((slot & 1) * 6, 6)]
            pltpu.make_async_copy(tile_ref.at[t], target, out_sem).start()

    tail_copy.wait()
    pltpu.make_async_copy(tile_ref, tile_ref, out_sem).wait()


def pack(owners, offsets, spline_index, spline_frac, projection, forces, device_count):
    hbm = pl.BlockSpec(memory_space=pltpu.HBM)
    tiles = owners.shape[0]
    return pl.pallas_call(
        pack_kernel,
        out_shape=jax.ShapeDtypeStruct((device_count, 13, 8, 128), BF16),
        in_specs=[hbm] * 6,
        out_specs=hbm,
        scratch_shapes=[
            pltpu.SMEM((tiles,), jnp.int32),
            pltpu.SMEM((tiles,), jnp.int32),
            pltpu.SMEM((device_count,), jnp.int32),
            pltpu.SMEM((tiles,), jnp.int32),
            pltpu.VMEM(spline_index.shape, spline_index.dtype),
            pltpu.VMEM(spline_frac.shape, BF16),
            pltpu.VMEM(projection.shape, BF16),
            pltpu.VMEM(forces.shape, BF16),
            pltpu.VMEM(forces.shape, F32),
            pltpu.VMEM((tiles, 6, 8, 128), BF16),
            pltpu.VMEM((device_count, 8, 128), F32),
            pltpu.VMEM((device_count, 8, 128), BF16),
            pltpu.SemaphoreType.DMA((3, CHUNKS)),
            pltpu.SemaphoreType.DMA,
            pltpu.SemaphoreType.DMA,
            pltpu.SemaphoreType.DMA,
            pltpu.SemaphoreType.DMA((2,)),
        ],
        compiler_params=pltpu.CompilerParams(vmem_limit_bytes=60 * MiB),
        name="pack",
    )(owners, offsets, spline_index, spline_frac, projection, forces)


def spline_rows(recv_ref, source, place, scale, bufs):
    base_buf, window_buf = bufs[0:2]
    pieces = [[], [], [], []]
    lows = []
    for g in range(2):
        index = recv_ref[source, place * 6 + g].astype(F32)
        t = recv_ref[source, place * 6 + 2 + g].astype(F32)
        q = recv_ref[source, place * 6 + 4 + g].astype(F32) * scale
        base_buf[g] = index * (1.0 / 8.0)
        lows.append((index.astype(jnp.int32) & 7).astype(F32))
        u = 1.0 - t
        t2 = t * t
        t3 = t2 * t
        pieces[0].append(q * (u * u * u))
        pieces[1].append(q * (3.0 * t3 - 6.0 * t2 + 4.0))
        pieces[2].append(q * (3.0 * (t + t2 - t3) + 1.0))
        pieces[3].append(q * t3)
    low = jnp.concatenate(lows, axis=0).astype(BF16)
    pieces = [jnp.concatenate(p, axis=0).astype(BF16) for p in pieces]
    starts = [low == k for k in range(8)]
    zero = jnp.zeros((16, 128), BF16)
    for k in range(8):
        value = zero
        for m in range(4):
            value = jnp.where(starts[(k - m) % 8], pieces[m], value)
        value = value.astype(F32)
        for g in range(2):
            window_buf[g, pl.ds(k, 8, stride=8), :] = value[g * 8 : g * 8 + 8]


def build_design(bufs):
    base_buf, window_buf, design_buf = bufs[0:3]
    k = (lax.broadcasted_iota(jnp.int32, (16, 128), 0) & 7).astype(F32)
    shift = (k * (1.0 / 8.0) - 7.0 / 16.0).astype(BF16)
    zero = jnp.zeros((16, 128), BF16)
    for s in range(2):
        blocks = [None] * 16
        for n in range(4):
            row = s * 4 + n
            base = [base_buf[g, pl.ds(row, 8, stride=0), :] for g in range(2)]
            base = jnp.concatenate(base, axis=0).astype(BF16)
            home = (base - shift) + 128
            window = [window_buf[g, row * 8 : row * 8 + 8, :] for g in range(2)]
            window = jnp.concatenate(window, axis=0).astype(BF16)
            for b in range(16):
                piece = jnp.where(home == 128 + b, window, zero)
                blocks[b] = piece if n == 0 else blocks[b] + piece
        for b in range(16):
            at = s * 128 + b * 8
            design_buf[at : at + 8, 0:128] = blocks[b][0:8]
            design_buf[at : at + 8, 128:256] = blocks[b][8:16]


def force_rows(recv_ref, source, place, bufs):
    design_buf, force_buf = bufs[2:4]
    force_buf[...] = recv_ref[source, 12].astype(F32)
    first = lax.broadcasted_iota(jnp.int32, (16, 128), 0) == 0
    rows = []
    for g in range(2):
        row = force_buf[pl.ds(place * 2 + g, 8, stride=0), :]
        row = jnp.concatenate([row, row], axis=0)
        rows.append(jnp.where(first, row, 0.0).astype(BF16))
    design_buf[256:272, :] = jnp.concatenate(rows, axis=1)


def build_tile(recv_ref, word, scale, bufs):
    source = (word >> 1) & 127
    place = word & 1
    spline_rows(recv_ref, source, place, scale, bufs)
    force_rows(recv_ref, source, place, bufs)
    build_design(bufs)


def products(bufs):
    design_buf = bufs[2]
    return lax.dot_general(
        design_buf[...], design_buf[0:256, :], (((1,), (1,)), ((), ())), preferred_element_type=F32
    )


def sweep(count, word_at, recv_ref, add, bufs):
    sets = [bufs[u * 4 : u * 4 + 4] for u in range(GROUP)]
    for group in sets:
        group[2][...] = jnp.zeros_like(group[2])

    def clamped(i):
        return word_at(jnp.clip(i, 0, count - 1))

    def step(j, carry):
        first = j * GROUP
        for u in range(GROUP):
            out = products(sets[u])
            i = first + u
            scale = jnp.where(i < count, 1.0 / 6.0, 0.0).astype(F32)
            build_tile(recv_ref, clamped(i), scale, sets[u])
            add(clamped(i - GROUP), out)
        return carry

    turns = (count + GROUP - 1) // GROUP
    lax.fori_loop(0, turns, step, 0)

    @pl.when(count > 0)
    def _():
        for u in range(GROUP):
            add(clamped((turns - 1) * GROUP + u), products(sets[u]))


def edge_kernel(
    recv_ref, band_ref, rhs_ref, spill_ref, list_ref, meta_i32, first_words, second_words, edge_count,
    other_count, meta_sems, *bufs,
):
    counts = (edge_count, other_count)
    devices = recv_ref.shape[0]
    totals = [jnp.zeros((8, 128), F32)] * 4
    for d in range(devices):
        totals[d % 4] = totals[d % 4] + recv_ref[d, 12].astype(F32)
    mark = (totals[0] + totals[1] + totals[2] + totals[3])[4 : 4 + CAP]
    at_edge = mark == BLK_DEV
    other = (mark > 0) & (mark < BLK_DEV)
    kinds = jnp.concatenate([at_edge.astype(F32), other.astype(F32), jnp.zeros((4, 128), F32)], axis=0)
    ahead = lax.broadcasted_iota(jnp.int32, (128, 128), 0) < lax.broadcasted_iota(jnp.int32, (128, 128), 1)
    rank = lax.dot_general(
        kinds.astype(BF16), ahead.astype(F32).astype(BF16), (((1,), (0,)), ((), ())), preferred_element_type=F32
    )
    sums = jnp.sum(kinds, axis=1, keepdims=True)
    rank_edge = jnp.concatenate([rank[0:1], rank[1:2] + sums[0:1]], axis=0)
    rank_other = jnp.concatenate([rank[2:3], rank[3:4] + sums[2:3]], axis=0)
    slots = devices * CAP
    where_to = jnp.where(at_edge, rank_edge, jnp.where(other, slots - 1 - rank_other, slots)).astype(jnp.int32)
    shape = (CAP, 128)
    code = lax.broadcasted_iota(jnp.int32, shape, 1) * CAP + lax.broadcasted_iota(jnp.int32, shape, 0)
    meta_i32[0:CAP] = where_to * 65536 + mark.astype(jnp.int32) * 256 + code
    meta_i32[2:3] = jnp.broadcast_to(sums[0:1] + sums[1:2], (1, 128)).astype(jnp.int32)
    meta_i32[3:4] = jnp.broadcast_to(sums[2:3] + sums[3:4], (1, 128)).astype(jnp.int32)
    words = (first_words, second_words)
    copies = [pltpu.make_async_copy(meta_i32.at[k], ref, meta_sems.at[k]) for k, ref in enumerate(words + tuple(counts))]
    for copy in copies:
        copy.start()
    band_ref[...] = jnp.zeros_like(band_ref)
    rhs_ref[...] = jnp.zeros_like(rhs_ref)
    spill_ref[...] = jnp.zeros_like(spill_ref)
    for copy in copies:
        copy.wait()

    @pl.loop(0, devices, unroll=8)
    def _(d):
        for q in range(CAP):
            word = words[q][d]
            list_ref[word >> 16] = word

    list_ref[slots + 1] = counts[1][0]

    def add(word, out):
        band_ref[0] += out[0:128, 0:128]
        band_ref[1] += out[0:128, 128:256]
        spill_ref[0:128, :] += out[128:256, 128:256]
        rhs_ref[...] += out[256:264, 0:128]
        spill_ref[128:136, :] += out[256:264, 128:256]

    sweep(counts[0][0], lambda i: list_ref[i], recv_ref, add, bufs)


def inner_kernel(list_hbm, recv_ref, edge_band_ref, edge_rhs_ref, band_ref, rhs_ref, list_ref, list_sem, *bufs):
    list_copy = pltpu.make_async_copy(list_hbm, list_ref, list_sem)
    list_copy.start()
    slots = recv_ref.shape[0] * CAP
    last = band_ref.shape[0] - 1
    band_ref[0:last] = jnp.zeros((last, 2, 128, 128), F32)
    band_ref[last] = edge_band_ref[...]
    rhs_ref[...] = jnp.zeros_like(rhs_ref)
    rhs_ref[last:last + 1] = edge_rhs_ref[0:1, :]

    def add(word, out):
        at = ((word >> 8) & 255) - 1
        band_ref[at, 0] += out[0:128, 0:128]
        band_ref[at, 1] += out[0:128, 128:256]
        band_ref[at + 1, 0] += out[128:256, 128:256]
        rhs_ref[pl.ds(at, 1), :] += out[256:257, 0:128]
        rhs_ref[pl.ds(at + 1, 1), :] += out[256:257, 128:256]

    list_copy.wait()
    sweep(list_ref[slots + 1], lambda i: list_ref[slots - 1 - i], recv_ref, add, bufs)


def finish_kernel(band_ref, rhs_ref, spill_ref, band_hbm, rhs_hbm, first_band, first_rhs, sems):
    rest = pltpu.make_async_copy(band_ref.at[1:], band_hbm.at[1:], sems.at[0])
    lag = pltpu.make_async_copy(band_ref.at[0, 1], band_hbm.at[0, 1], sems.at[1])
    rest.start()
    lag.start()
    first_band[...] = band_ref[0, 0] + spill_ref[0:128, :]
    first_rhs[...] = rhs_ref[...]
    first_rhs[0:1, :] = rhs_ref[0:1, :] + spill_ref[128:129, :]
    diagonal = pltpu.make_async_copy(first_band, band_hbm.at[0, 0], sems.at[2])
    right = pltpu.make_async_copy(first_rhs, rhs_hbm, sems.at[3])
    diagonal.start()
    right.start()
    right.wait()
    diagonal.wait()
    lag.wait()
    rest.wait()


def buffers():
    return [
        pltpu.VMEM((2, 8, 128), F32),
        pltpu.VMEM((2, 64, 128), F32),
        pltpu.VMEM((272, 256), BF16),
        pltpu.VMEM((8, 128), F32),
    ] * GROUP


VMEM = pl.BlockSpec(memory_space=pltpu.VMEM)
SMEM = pl.BlockSpec(memory_space=pltpu.SMEM)
HBM = pl.BlockSpec(memory_space=pltpu.HBM)
SWEEP_COST = pl.CostEstimate(flops=4 << 30, bytes_accessed=4 << 20, transcendentals=0)


def edge(received):
    devices = received.shape[0]
    return pl.pallas_call(
        edge_kernel,
        out_shape=(
            jax.ShapeDtypeStruct((2, 128, 128), F32),
            jax.ShapeDtypeStruct((8, 128), F32),
            jax.ShapeDtypeStruct((136, 128), F32),
            jax.ShapeDtypeStruct((devices * CAP + 8,), jnp.int32),
        ),
        in_specs=[VMEM],
        out_specs=(VMEM, VMEM, VMEM, SMEM),
        scratch_shapes=[
            pltpu.VMEM((8, 128), jnp.int32),
            pltpu.SMEM((128,), jnp.int32),
            pltpu.SMEM((128,), jnp.int32),
            pltpu.SMEM((128,), jnp.int32),
            pltpu.SMEM((128,), jnp.int32),
            pltpu.SemaphoreType.DMA((4,)),
        ]
        + buffers(),
        compiler_params=pltpu.CompilerParams(vmem_limit_bytes=40 * MiB),
        cost_estimate=SWEEP_COST,
        name="edge",
    )(received)


def inner(lists, received, edge_band, edge_rhs):
    return pl.pallas_call(
        inner_kernel,
        out_shape=(
            jax.ShapeDtypeStruct((BLK_DEV, 2, 128, 128), F32),
            jax.ShapeDtypeStruct((BLK_DEV, 128), F32),
        ),
        in_specs=[HBM, VMEM, VMEM, VMEM],
        out_specs=(VMEM, VMEM),
        scratch_shapes=[pltpu.SMEM(lists.shape, jnp.int32), pltpu.SemaphoreType.DMA] + buffers(),
        compiler_params=pltpu.CompilerParams(vmem_limit_bytes=40 * MiB),
        cost_estimate=SWEEP_COST,
        name="inner",
    )(lists, received, edge_band, edge_rhs)


def finish(band, rhs, spill):
    return pl.pallas_call(
        finish_kernel,
        out_shape=(jax.ShapeDtypeStruct(band.shape, F32), jax.ShapeDtypeStruct(rhs.shape, F32)),
        in_specs=[VMEM, VMEM, VMEM],
        out_specs=(HBM, HBM),
        scratch_shapes=[
            pltpu.VMEM((128, 128), F32),
            pltpu.VMEM(rhs.shape, F32),
            pltpu.SemaphoreType.DMA((4,)),
        ],
        compiler_params=pltpu.CompilerParams(vmem_limit_bytes=16 * MiB),
        name="finish",
    )(band, rhs, spill)


def on_device(spline_index, spline_frac, projection, forces, row_owner, row_offset):
    device_count = lax.axis_size(AXES)
    sent = pack(row_owner[:, 0], row_offset, spline_index, spline_frac, projection, forces, device_count)
    received = lax.all_to_all(sent, AXES, split_axis=0, concat_axis=0, tiled=True)
    edge_band, edge_rhs, spill, lists = edge(received)
    route = [(i, (i + 1) % device_count) for i in range(device_count)]
    spill = lax.ppermute(spill, AXES, route)
    band, rhs = inner(lists, received, edge_band, edge_rhs)
    return finish(band, rhs, spill)


def solution(mesh):
    in_specs = (
        P(AXES, None, None, None),
        P(AXES, None, None, None),
        P(AXES, None, None, None),
        P(AXES, None),
        P(AXES, None),
        P(AXES),
    )
    out_specs = (P(AXES, None, None, None), P(AXES, None))
    return jax.shard_map(
        on_device, mesh=mesh, in_specs=in_specs, out_specs=out_specs, check_vma=False
    )
```

```python
import jax
import jax.numpy as jnp
from jax import lax
from jax.experimental import pallas as pl
from jax.experimental.pallas import tpu as pltpu
from jax.sharding import PartitionSpec as P

CO = 128
BLK_DEV = 22
CAP = 2
AXES = ("frame", "panel")
BF16 = jnp.bfloat16
F32 = jnp.float32
CHUNKS = 2
GROUP = 8
MiB = 1 << 20


def pack_kernel(
    owner_hbm, offset_hbm, index_hbm, frac_hbm, proj_hbm, force_hbm, out_hbm,
    owner_ref, offset_ref, count_ref, slot_ref, index_ref, frac_ref, proj_ref, force_ref, force_f32, tile_ref, tail_f32, tail_ref,
    in_sems, force_sem, out_sem, tail_sem, row_sems,
):
    device_count = out_hbm.shape[0]
    tiles = owner_ref.shape[0]
    step = tiles // CHUNKS
    arrays = ((index_hbm, index_ref), (frac_hbm, frac_ref), (proj_hbm, proj_ref))

    def fetch(a, c):
        part = pl.ds(c * step, step)
        return pltpu.make_async_copy(arrays[a][0].at[part], arrays[a][1].at[part], in_sems.at[a, c])

    force_copy = pltpu.make_async_copy(force_hbm, force_ref, force_sem)
    owner_copy = pltpu.make_async_copy(owner_hbm, owner_ref, row_sems.at[0])
    offset_copy = pltpu.make_async_copy(offset_hbm, offset_ref, row_sems.at[1])
    force_copy.start()
    owner_copy.start()
    offset_copy.start()
    for c in range(CHUNKS):
        for a in range(3):
            fetch(a, c).start()

    @pl.loop(0, device_count, unroll=8)
    def _(d):
        count_ref[d] = 0

    tail_f32[...] = jnp.zeros_like(tail_f32)
    me = lax.axis_index(AXES[0]) * lax.axis_size(AXES[1]) + lax.axis_index(AXES[1])
    here = lax.broadcasted_iota(jnp.int32, (1, 128), 1) == me
    owner_copy.wait()
    offset_copy.wait()
    force_copy.wait()
    force_f32[...] = force_ref[...].astype(F32)

    @pl.loop(0, tiles, unroll=4)
    def _(t):
        owner = owner_ref[t]
        place = count_ref[owner]
        count_ref[owner] = place + 1
        slot_ref[t] = owner * CAP + place
        row = force_f32[pl.ds(t, 1), :]
        for g in range(2):
            tail_f32[owner, pl.ds(place * 2 + g, 1), :] = row[:, g * 128 : g * 128 + 128]
        tail_f32[owner, pl.ds(4 + place, 1), :] = jnp.where(here, (offset_ref[t] + 1).astype(F32), 0.0)

    tail_ref[...] = tail_f32[...].astype(BF16)
    tail_copy = pltpu.make_async_copy(tail_ref, out_hbm.at[:, 12], tail_sem)
    tail_copy.start()

    for c in range(CHUNKS):
        for a in range(3):
            fetch(a, c).wait()

        @pl.loop(c * step, (c + 1) * step, unroll=4)
        def _(t):
            slot = slot_ref[t]
            for a in range(3):
                ref = arrays[a][1]
                for g in range(2):
                    low = ref[t, 0, :, g * 128 : g * 128 + 128].astype(F32)
                    high = ref[t, 1, :, g * 128 : g * 128 + 128].astype(F32)
                    tile_ref[t, a * 2 + g] = jnp.concatenate([low, high], axis=0).astype(BF16)
            target = out_hbm.at[slot >> 1, pl.ds((slot & 1) * 6, 6)]
            pltpu.make_async_copy(tile_ref.at[t], target, out_sem).start()

    tail_copy.wait()
    pltpu.make_async_copy(tile_ref, tile_ref, out_sem).wait()


def pack(owners, offsets, spline_index, spline_frac, projection, forces, device_count):
    hbm = pl.BlockSpec(memory_space=pltpu.HBM)
    tiles = owners.shape[0]
    return pl.pallas_call(
        pack_kernel,
        out_shape=jax.ShapeDtypeStruct((device_count, 13, 8, 128), BF16),
        in_specs=[hbm] * 6,
        out_specs=hbm,
        scratch_shapes=[
            pltpu.SMEM((tiles,), jnp.int32),
            pltpu.SMEM((tiles,), jnp.int32),
            pltpu.SMEM((device_count,), jnp.int32),
            pltpu.SMEM((tiles,), jnp.int32),
            pltpu.VMEM(spline_index.shape, spline_index.dtype),
            pltpu.VMEM(spline_frac.shape, BF16),
            pltpu.VMEM(projection.shape, BF16),
            pltpu.VMEM(forces.shape, BF16),
            pltpu.VMEM(forces.shape, F32),
            pltpu.VMEM((tiles, 6, 8, 128), BF16),
            pltpu.VMEM((device_count, 8, 128), F32),
            pltpu.VMEM((device_count, 8, 128), BF16),
            pltpu.SemaphoreType.DMA((3, CHUNKS)),
            pltpu.SemaphoreType.DMA,
            pltpu.SemaphoreType.DMA,
            pltpu.SemaphoreType.DMA,
            pltpu.SemaphoreType.DMA((2,)),
        ],
        compiler_params=pltpu.CompilerParams(vmem_limit_bytes=60 * MiB),
        name="pack",
    )(owners, offsets, spline_index, spline_frac, projection, forces)


def spline_rows(recv_ref, source, place, scale, bufs):
    base_buf, window_buf = bufs[0:2]
    pieces = [[], [], [], []]
    lows = []
    for g in range(2):
        index = recv_ref[source, place * 6 + g].astype(F32)
        t = recv_ref[source, place * 6 + 2 + g].astype(F32)
        q = recv_ref[source, place * 6 + 4 + g].astype(F32) * scale
        base_buf[g] = index * (1.0 / 8.0)
        lows.append((index.astype(jnp.int32) & 7).astype(F32))
        u = 1.0 - t
        t2 = t * t
        t3 = t2 * t
        pieces[0].append(q * (u * u * u))
        pieces[1].append(q * (3.0 * t3 - 6.0 * t2 + 4.0))
        pieces[2].append(q * (3.0 * (t + t2 - t3) + 1.0))
        pieces[3].append(q * t3)
    low = jnp.concatenate(lows, axis=0).astype(BF16)
    pieces = [jnp.concatenate(p, axis=0).astype(BF16) for p in pieces]
    starts = [low == k for k in range(8)]
    zero = jnp.zeros((16, 128), BF16)
    for k in range(8):
        value = zero
        for m in range(4):
            value = jnp.where(starts[(k - m) % 8], pieces[m], value)
        value = value.astype(F32)
        for g in range(2):
            window_buf[g, pl.ds(k, 8, stride=8), :] = value[g * 8 : g * 8 + 8]


def build_design(bufs):
    base_buf, window_buf, design_buf = bufs[0:3]
    k = (lax.broadcasted_iota(jnp.int32, (16, 128), 0) & 7).astype(F32)
    shift = (k * (1.0 / 8.0) - 7.0 / 16.0).astype(BF16)
    zero = jnp.zeros((16, 128), BF16)
    for s in range(2):
        homes, alone, windows = [], [], []
        for n in range(4):
            row = s * 4 + n
            base = [base_buf[g, pl.ds(row, 8, stride=0), :] for g in range(2)]
            base = jnp.concatenate(base, axis=0).astype(BF16)
            home = (base - shift) + 128
            window = [window_buf[g, row * 8 : row * 8 + 8, :] for g in range(2)]
            window = jnp.concatenate(window, axis=0).astype(BF16)
            merged = window
            for p in range(n):
                merged = merged + jnp.where(homes[p] == home, alone[p], zero)
            homes.append(home)
            alone.append(window)
            windows.append(merged)
        for b in range(16):
            block = zero
            for n in range(4):
                block = jnp.where(homes[n] == 128 + b, windows[n], block)
            at = s * 128 + b * 8
            design_buf[at : at + 8, 0:128] = block[0:8]
            design_buf[at : at + 8, 128:256] = block[8:16]


def force_rows(recv_ref, source, place, bufs):
    design_buf, force_buf = bufs[2:4]
    force_buf[...] = recv_ref[source, 12].astype(F32)
    first = lax.broadcasted_iota(jnp.int32, (16, 128), 0) == 0
    rows = []
    for g in range(2):
        row = force_buf[pl.ds(place * 2 + g, 8, stride=0), :]
        row = jnp.concatenate([row, row], axis=0)
        rows.append(jnp.where(first, row, 0.0).astype(BF16))
    design_buf[256:272, :] = jnp.concatenate(rows, axis=1)


def build_tile(recv_ref, word, scale, bufs):
    source = (word >> 1) & 127
    place = word & 1
    spline_rows(recv_ref, source, place, scale, bufs)
    force_rows(recv_ref, source, place, bufs)
    build_design(bufs)


def products(bufs):
    design_buf = bufs[2]

    def times(rows, columns):
        return lax.dot_general(rows, columns, (((1,), (1,)), ((), ())), preferred_element_type=F32)

    rows = jnp.concatenate([design_buf[0:128], design_buf[256:272]], axis=0)
    return times(rows, design_buf[0:128]), times(design_buf[...], design_buf[128:256])


def sweep(count, word_at, recv_ref, add, bufs):
    sets = [bufs[u * 4 : u * 4 + 4] for u in range(GROUP)]
    for group in sets:
        group[2][...] = jnp.zeros_like(group[2])

    def clamped(i):
        return word_at(jnp.clip(i, 0, count - 1))

    def step(j, carry):
        first = j * GROUP
        for u in range(GROUP):
            out = products(sets[u])
            i = first + u
            scale = jnp.where(i < count, 1.0 / 6.0, 0.0).astype(F32)
            build_tile(recv_ref, clamped(i), scale, sets[u])
            add(clamped(i - GROUP), out)
        return carry

    turns = (count + GROUP - 1) // GROUP
    lax.fori_loop(0, turns, step, 0)

    @pl.when(count > 0)
    def _():
        for u in range(GROUP):
            add(clamped((turns - 1) * GROUP + u), products(sets[u]))


def edge_kernel(
    recv_ref, band_ref, rhs_ref, spill_ref, list_ref, meta_i32, first_words, second_words, edge_count,
    other_count, meta_sems, *bufs,
):
    counts = (edge_count, other_count)
    devices = recv_ref.shape[0]
    totals = [jnp.zeros((8, 128), F32)] * 4
    for d in range(devices):
        totals[d % 4] = totals[d % 4] + recv_ref[d, 12].astype(F32)
    mark = (totals[0] + totals[1] + totals[2] + totals[3])[4 : 4 + CAP]
    at_edge = mark == BLK_DEV
    other = (mark > 0) & (mark < BLK_DEV)
    kinds = jnp.concatenate([at_edge.astype(F32), other.astype(F32), jnp.zeros((4, 128), F32)], axis=0)
    ahead = lax.broadcasted_iota(jnp.int32, (128, 128), 0) < lax.broadcasted_iota(jnp.int32, (128, 128), 1)
    rank = lax.dot_general(
        kinds.astype(BF16), ahead.astype(F32).astype(BF16), (((1,), (0,)), ((), ())), preferred_element_type=F32
    )
    sums = jnp.sum(kinds, axis=1, keepdims=True)
    rank_edge = jnp.concatenate([rank[0:1], rank[1:2] + sums[0:1]], axis=0)
    rank_other = jnp.concatenate([rank[2:3], rank[3:4] + sums[2:3]], axis=0)
    slots = devices * CAP
    where_to = jnp.where(at_edge, rank_edge, jnp.where(other, slots - 1 - rank_other, slots)).astype(jnp.int32)
    shape = (CAP, 128)
    code = lax.broadcasted_iota(jnp.int32, shape, 1) * CAP + lax.broadcasted_iota(jnp.int32, shape, 0)
    meta_i32[0:CAP] = where_to * 65536 + mark.astype(jnp.int32) * 256 + code
    meta_i32[2:3] = jnp.broadcast_to(sums[0:1] + sums[1:2], (1, 128)).astype(jnp.int32)
    meta_i32[3:4] = jnp.broadcast_to(sums[2:3] + sums[3:4], (1, 128)).astype(jnp.int32)
    words = (first_words, second_words)
    copies = [pltpu.make_async_copy(meta_i32.at[k], ref, meta_sems.at[k]) for k, ref in enumerate(words + tuple(counts))]
    for copy in copies:
        copy.start()
    band_ref[...] = jnp.zeros_like(band_ref)
    rhs_ref[...] = jnp.zeros_like(rhs_ref)
    spill_ref[...] = jnp.zeros_like(spill_ref)
    for copy in copies:
        copy.wait()

    @pl.loop(0, devices, unroll=8)
    def _(d):
        for q in range(CAP):
            word = words[q][d]
            list_ref[word >> 16] = word

    list_ref[slots + 1] = counts[1][0]

    def add(word, out):
        left, right = out
        band_ref[0] += left[0:128]
        band_ref[1] += right[0:128]
        spill_ref[0:128, :] += right[128:256]
        rhs_ref[...] += left[128:136]
        spill_ref[128:136, :] += right[256:264]

    sweep(counts[0][0], lambda i: list_ref[i], recv_ref, add, bufs)


def inner_kernel(list_hbm, recv_ref, edge_band_ref, edge_rhs_ref, band_ref, rhs_ref, list_ref, list_sem, *bufs):
    list_copy = pltpu.make_async_copy(list_hbm, list_ref, list_sem)
    list_copy.start()
    slots = recv_ref.shape[0] * CAP
    last = band_ref.shape[0] - 1
    band_ref[0:last] = jnp.zeros((last, 2, 128, 128), F32)
    band_ref[last] = edge_band_ref[...]
    rhs_ref[...] = jnp.zeros_like(rhs_ref)
    rhs_ref[last:last + 1] = edge_rhs_ref[0:1, :]

    def add(word, out):
        at = ((word >> 8) & 255) - 1
        left, right = out
        band_ref[at, 0] += left[0:128]
        band_ref[at, 1] += right[0:128]
        band_ref[at + 1, 0] += right[128:256]
        rhs_ref[pl.ds(at, 1), :] += left[128:129]
        rhs_ref[pl.ds(at + 1, 1), :] += right[256:257]

    list_copy.wait()
    sweep(list_ref[slots + 1], lambda i: list_ref[slots - 1 - i], recv_ref, add, bufs)


def finish_kernel(band_ref, rhs_ref, spill_ref, band_hbm, rhs_hbm, first_band, first_rhs, sems):
    rest = pltpu.make_async_copy(band_ref.at[1:], band_hbm.at[1:], sems.at[0])
    lag = pltpu.make_async_copy(band_ref.at[0, 1], band_hbm.at[0, 1], sems.at[1])
    rest.start()
    lag.start()
    first_band[...] = band_ref[0, 0] + spill_ref[0:128, :]
    first_rhs[...] = rhs_ref[...]
    first_rhs[0:1, :] = rhs_ref[0:1, :] + spill_ref[128:129, :]
    diagonal = pltpu.make_async_copy(first_band, band_hbm.at[0, 0], sems.at[2])
    right = pltpu.make_async_copy(first_rhs, rhs_hbm, sems.at[3])
    diagonal.start()
    right.start()
    right.wait()
    diagonal.wait()
    lag.wait()
    rest.wait()


def buffers():
    return [
        pltpu.VMEM((2, 8, 128), F32),
        pltpu.VMEM((2, 64, 128), F32),
        pltpu.VMEM((272, 256), BF16),
        pltpu.VMEM((8, 128), F32),
    ] * GROUP


VMEM = pl.BlockSpec(memory_space=pltpu.VMEM)
SMEM = pl.BlockSpec(memory_space=pltpu.SMEM)
HBM = pl.BlockSpec(memory_space=pltpu.HBM)
SWEEP_COST = pl.CostEstimate(flops=4 << 30, bytes_accessed=4 << 20, transcendentals=0)


def edge(received):
    devices = received.shape[0]
    return pl.pallas_call(
        edge_kernel,
        out_shape=(
            jax.ShapeDtypeStruct((2, 128, 128), F32),
            jax.ShapeDtypeStruct((8, 128), F32),
            jax.ShapeDtypeStruct((136, 128), F32),
            jax.ShapeDtypeStruct((devices * CAP + 8,), jnp.int32),
        ),
        in_specs=[VMEM],
        out_specs=(VMEM, VMEM, VMEM, SMEM),
        scratch_shapes=[
            pltpu.VMEM((8, 128), jnp.int32),
            pltpu.SMEM((128,), jnp.int32),
            pltpu.SMEM((128,), jnp.int32),
            pltpu.SMEM((128,), jnp.int32),
            pltpu.SMEM((128,), jnp.int32),
            pltpu.SemaphoreType.DMA((4,)),
        ]
        + buffers(),
        compiler_params=pltpu.CompilerParams(vmem_limit_bytes=40 * MiB),
        cost_estimate=SWEEP_COST,
        name="edge",
    )(received)


def inner(lists, received, edge_band, edge_rhs):
    return pl.pallas_call(
        inner_kernel,
        out_shape=(
            jax.ShapeDtypeStruct((BLK_DEV, 2, 128, 128), F32),
            jax.ShapeDtypeStruct((BLK_DEV, 128), F32),
        ),
        in_specs=[HBM, VMEM, VMEM, VMEM],
        out_specs=(VMEM, VMEM),
        scratch_shapes=[pltpu.SMEM(lists.shape, jnp.int32), pltpu.SemaphoreType.DMA] + buffers(),
        compiler_params=pltpu.CompilerParams(vmem_limit_bytes=40 * MiB),
        cost_estimate=SWEEP_COST,
        name="inner",
    )(lists, received, edge_band, edge_rhs)


def finish(band, rhs, spill):
    return pl.pallas_call(
        finish_kernel,
        out_shape=(jax.ShapeDtypeStruct(band.shape, F32), jax.ShapeDtypeStruct(rhs.shape, F32)),
        in_specs=[VMEM, VMEM, VMEM],
        out_specs=(HBM, HBM),
        scratch_shapes=[
            pltpu.VMEM((128, 128), F32),
            pltpu.VMEM(rhs.shape, F32),
            pltpu.SemaphoreType.DMA((4,)),
        ],
        compiler_params=pltpu.CompilerParams(vmem_limit_bytes=16 * MiB),
        name="finish",
    )(band, rhs, spill)


def on_device(spline_index, spline_frac, projection, forces, row_owner, row_offset):
    device_count = lax.axis_size(AXES)
    sent = pack(row_owner[:, 0], row_offset, spline_index, spline_frac, projection, forces, device_count)
    received = lax.all_to_all(sent, AXES, split_axis=0, concat_axis=0, tiled=True)
    edge_band, edge_rhs, spill, lists = edge(received)
    route = [(i, (i + 1) % device_count) for i in range(device_count)]
    spill = lax.ppermute(spill, AXES, route)
    band, rhs = inner(lists, received, edge_band, edge_rhs)
    return finish(band, rhs, spill)


def solution(mesh):
    in_specs = (
        P(AXES, None, None, None),
        P(AXES, None, None, None),
        P(AXES, None, None, None),
        P(AXES, None),
        P(AXES, None),
        P(AXES),
    )
    out_specs = (P(AXES, None, None, None), P(AXES, None))
    return jax.shard_map(
        on_device, mesh=mesh, in_specs=in_specs, out_specs=out_specs, check_vma=False
    )
```

```python
import jax
import jax.numpy as jnp
from jax import lax
from jax.experimental import pallas as pl
from jax.experimental.pallas import tpu as pltpu
from jax.sharding import PartitionSpec as P

CO = 128
BLK_DEV = 22
CAP = 2
AXES = ("frame", "panel")
BF16 = jnp.bfloat16
F32 = jnp.float32
CHUNKS = 2
GROUP = 8
MiB = 1 << 20


def pack_kernel(
    owner_hbm, offset_hbm, index_hbm, frac_hbm, proj_hbm, force_hbm, out_hbm,
    owner_ref, offset_ref, count_ref, slot_ref, index_ref, frac_ref, proj_ref, force_ref, force_f32, tile_ref, tail_f32, tail_ref,
    in_sems, force_sem, out_sem, tail_sem, row_sems,
):
    device_count = out_hbm.shape[0]
    tiles = owner_ref.shape[0]
    step = tiles // CHUNKS
    arrays = ((index_hbm, index_ref), (frac_hbm, frac_ref), (proj_hbm, proj_ref))

    def fetch(a, c):
        part = pl.ds(c * step, step)
        return pltpu.make_async_copy(arrays[a][0].at[part], arrays[a][1].at[part], in_sems.at[a, c])

    force_copy = pltpu.make_async_copy(force_hbm, force_ref, force_sem)
    owner_copy = pltpu.make_async_copy(owner_hbm, owner_ref, row_sems.at[0])
    offset_copy = pltpu.make_async_copy(offset_hbm, offset_ref, row_sems.at[1])
    force_copy.start()
    owner_copy.start()
    offset_copy.start()
    for c in range(CHUNKS):
        for a in range(3):
            fetch(a, c).start()

    @pl.loop(0, device_count, unroll=8)
    def _(d):
        count_ref[d] = 0

    tail_f32[...] = jnp.zeros_like(tail_f32)
    me = lax.axis_index(AXES[0]) * lax.axis_size(AXES[1]) + lax.axis_index(AXES[1])
    here = lax.broadcasted_iota(jnp.int32, (1, 128), 1) == me
    owner_copy.wait()
    offset_copy.wait()
    force_copy.wait()
    force_f32[...] = force_ref[...].astype(F32)

    @pl.loop(0, tiles, unroll=4)
    def _(t):
        owner = owner_ref[t]
        place = count_ref[owner]
        count_ref[owner] = place + 1
        slot_ref[t] = owner * CAP + place
        row = force_f32[pl.ds(t, 1), :]
        for g in range(2):
            tail_f32[owner, pl.ds(place * 2 + g, 1), :] = row[:, g * 128 : g * 128 + 128]
        tail_f32[owner, pl.ds(4 + place, 1), :] = jnp.where(here, (offset_ref[t] + 1).astype(F32), 0.0)

    tail_ref[...] = tail_f32[...].astype(BF16)
    tail_copy = pltpu.make_async_copy(tail_ref, out_hbm.at[:, 12], tail_sem)
    tail_copy.start()

    for c in range(CHUNKS):
        for a in range(3):
            fetch(a, c).wait()

        @pl.loop(c * step, (c + 1) * step, unroll=4)
        def _(t):
            slot = slot_ref[t]
            for a in range(3):
                ref = arrays[a][1]
                for g in range(2):
                    low = ref[t, 0, :, g * 128 : g * 128 + 128].astype(F32)
                    high = ref[t, 1, :, g * 128 : g * 128 + 128].astype(F32)
                    tile_ref[t, a * 2 + g] = jnp.concatenate([low, high], axis=0).astype(BF16)
            target = out_hbm.at[slot >> 1, pl.ds((slot & 1) * 6, 6)]
            pltpu.make_async_copy(tile_ref.at[t], target, out_sem).start()

    tail_copy.wait()
    pltpu.make_async_copy(tile_ref, tile_ref, out_sem).wait()


def pack(owners, offsets, spline_index, spline_frac, projection, forces, device_count):
    hbm = pl.BlockSpec(memory_space=pltpu.HBM)
    tiles = owners.shape[0]
    return pl.pallas_call(
        pack_kernel,
        out_shape=jax.ShapeDtypeStruct((device_count, 13, 8, 128), BF16),
        in_specs=[hbm] * 6,
        out_specs=hbm,
        scratch_shapes=[
            pltpu.SMEM((tiles,), jnp.int32),
            pltpu.SMEM((tiles,), jnp.int32),
            pltpu.SMEM((device_count,), jnp.int32),
            pltpu.SMEM((tiles,), jnp.int32),
            pltpu.VMEM(spline_index.shape, spline_index.dtype),
            pltpu.VMEM(spline_frac.shape, BF16),
            pltpu.VMEM(projection.shape, BF16),
            pltpu.VMEM(forces.shape, BF16),
            pltpu.VMEM(forces.shape, F32),
            pltpu.VMEM((tiles, 6, 8, 128), BF16),
            pltpu.VMEM((device_count, 8, 128), F32),
            pltpu.VMEM((device_count, 8, 128), BF16),
            pltpu.SemaphoreType.DMA((3, CHUNKS)),
            pltpu.SemaphoreType.DMA,
            pltpu.SemaphoreType.DMA,
            pltpu.SemaphoreType.DMA,
            pltpu.SemaphoreType.DMA((2,)),
        ],
        compiler_params=pltpu.CompilerParams(vmem_limit_bytes=60 * MiB),
        name="pack",
    )(owners, offsets, spline_index, spline_frac, projection, forces)


def spline_rows(recv_ref, source, place, scale, bufs):
    base_buf, window_buf = bufs[0:2]
    pieces = [[], [], [], []]
    lows = []
    for g in range(2):
        index = recv_ref[source, place * 6 + g].astype(F32)
        t = recv_ref[source, place * 6 + 2 + g].astype(F32)
        q = recv_ref[source, place * 6 + 4 + g].astype(F32) * scale
        base_buf[g] = index * (1.0 / 8.0)
        lows.append((index.astype(jnp.int32) & 7).astype(F32))
        u = 1.0 - t
        t2 = t * t
        t3 = t2 * t
        pieces[0].append(q * (u * u * u))
        pieces[1].append(q * (3.0 * t3 - 6.0 * t2 + 4.0))
        pieces[2].append(q * (3.0 * (t + t2 - t3) + 1.0))
        pieces[3].append(q * t3)
    low = jnp.concatenate(lows, axis=0).astype(BF16)
    pieces = [jnp.concatenate(p, axis=0).astype(BF16) for p in pieces]
    starts = [low == k for k in range(8)]
    zero = jnp.zeros((16, 128), BF16)
    for k in range(8):
        value = zero
        for m in range(4):
            value = jnp.where(starts[(k - m) % 8], pieces[m], value)
        value = value.astype(F32)
        for g in range(2):
            window_buf[g, pl.ds(k, 8, stride=8), :] = value[g * 8 : g * 8 + 8]


def build_design(bufs):
    base_buf, window_buf, design_buf = bufs[0:3]
    k = (lax.broadcasted_iota(jnp.int32, (16, 128), 0) & 7).astype(F32)
    shift = (k * (1.0 / 8.0) - 7.0 / 16.0).astype(BF16)
    zero = jnp.zeros((16, 128), BF16)
    for s in range(2):
        homes, alone, windows = [], [], []
        for n in range(4):
            row = s * 4 + n
            base = [base_buf[g, pl.ds(row, 8, stride=0), :] for g in range(2)]
            base = jnp.concatenate(base, axis=0).astype(BF16)
            home = (base - shift) + 128
            window = [window_buf[g, row * 8 : row * 8 + 8, :] for g in range(2)]
            window = jnp.concatenate(window, axis=0).astype(BF16)
            merged = window
            for p in range(n):
                merged = merged + jnp.where(homes[p] == home, alone[p], zero)
            homes.append(home)
            alone.append(window)
            windows.append(merged)
        for b in range(16):
            block = zero
            for n in range(4):
                block = jnp.where(homes[n] == 128 + b, windows[n], block)
            at = s * 128 + b * 8
            design_buf[at : at + 8, 0:128] = block[0:8]
            design_buf[at : at + 8, 128:256] = block[8:16]


def force_rows(recv_ref, source, place, bufs):
    design_buf, force_buf = bufs[2:4]
    force_buf[...] = recv_ref[source, 12].astype(F32)
    first = lax.broadcasted_iota(jnp.int32, (16, 128), 0) == 0
    rows = []
    for g in range(2):
        row = force_buf[pl.ds(place * 2 + g, 8, stride=0), :]
        row = jnp.concatenate([row, row], axis=0)
        rows.append(jnp.where(first, row, 0.0).astype(BF16))
    design_buf[256:272, :] = jnp.concatenate(rows, axis=1)


def build_tile(recv_ref, word, scale, bufs):
    source = (word >> 1) & 127
    place = word & 1
    spline_rows(recv_ref, source, place, scale, bufs)
    force_rows(recv_ref, source, place, bufs)
    build_design(bufs)


def products(bufs):
    design_buf = bufs[2]

    def times(rows, columns):
        return lax.dot_general(rows, columns, (((1,), (1,)), ((), ())), preferred_element_type=F32)

    rows = jnp.concatenate([design_buf[0:128], design_buf[256:272]], axis=0)
    return times(rows, design_buf[0:128]), times(design_buf[...], design_buf[128:256])


def sweep(count, word_at, recv_ref, add, bufs):
    sets = [bufs[u * 4 : u * 4 + 4] for u in range(GROUP)]
    for group in sets:
        group[2][...] = jnp.zeros_like(group[2])

    def clamped(i):
        return word_at(jnp.clip(i, 0, count - 1))

    def step(j, carry):
        first = j * GROUP
        for u in range(GROUP):
            add(clamped(first + u - GROUP), products(sets[u]))
        for u in range(GROUP):
            i = first + u
            scale = jnp.where(i < count, 1.0 / 6.0, 0.0).astype(F32)
            build_tile(recv_ref, clamped(i), scale, sets[u])
        return carry

    turns = (count + GROUP - 1) // GROUP
    lax.fori_loop(0, turns, step, 0)

    @pl.when(count > 0)
    def _():
        for u in range(GROUP):
            add(clamped((turns - 1) * GROUP + u), products(sets[u]))


def edge_kernel(
    recv_ref, band_ref, rhs_ref, spill_ref, list_ref, meta_i32, first_words, second_words, edge_count,
    other_count, meta_sems, *bufs,
):
    counts = (edge_count, other_count)
    devices = recv_ref.shape[0]
    totals = [jnp.zeros((8, 128), F32)] * 4
    for d in range(devices):
        totals[d % 4] = totals[d % 4] + recv_ref[d, 12].astype(F32)
    mark = (totals[0] + totals[1] + totals[2] + totals[3])[4 : 4 + CAP]
    at_edge = mark == BLK_DEV
    other = (mark > 0) & (mark < BLK_DEV)
    kinds = jnp.concatenate([at_edge.astype(F32), other.astype(F32), jnp.zeros((4, 128), F32)], axis=0)
    ahead = lax.broadcasted_iota(jnp.int32, (128, 128), 0) < lax.broadcasted_iota(jnp.int32, (128, 128), 1)
    rank = lax.dot_general(
        kinds.astype(BF16), ahead.astype(F32).astype(BF16), (((1,), (0,)), ((), ())), preferred_element_type=F32
    )
    sums = jnp.sum(kinds, axis=1, keepdims=True)
    rank_edge = jnp.concatenate([rank[0:1], rank[1:2] + sums[0:1]], axis=0)
    rank_other = jnp.concatenate([rank[2:3], rank[3:4] + sums[2:3]], axis=0)
    slots = devices * CAP
    where_to = jnp.where(at_edge, rank_edge, jnp.where(other, slots - 1 - rank_other, slots)).astype(jnp.int32)
    shape = (CAP, 128)
    code = lax.broadcasted_iota(jnp.int32, shape, 1) * CAP + lax.broadcasted_iota(jnp.int32, shape, 0)
    meta_i32[0:CAP] = where_to * 65536 + mark.astype(jnp.int32) * 256 + code
    meta_i32[2:3] = jnp.broadcast_to(sums[0:1] + sums[1:2], (1, 128)).astype(jnp.int32)
    meta_i32[3:4] = jnp.broadcast_to(sums[2:3] + sums[3:4], (1, 128)).astype(jnp.int32)
    words = (first_words, second_words)
    copies = [pltpu.make_async_copy(meta_i32.at[k], ref, meta_sems.at[k]) for k, ref in enumerate(words + tuple(counts))]
    for copy in copies:
        copy.start()
    band_ref[...] = jnp.zeros_like(band_ref)
    rhs_ref[...] = jnp.zeros_like(rhs_ref)
    spill_ref[...] = jnp.zeros_like(spill_ref)
    for copy in copies:
        copy.wait()

    @pl.loop(0, devices, unroll=8)
    def _(d):
        for q in range(CAP):
            word = words[q][d]
            list_ref[word >> 16] = word

    list_ref[slots + 1] = counts[1][0]

    def add(word, out):
        left, right = out
        band_ref[0] += left[0:128]
        band_ref[1] += right[0:128]
        spill_ref[0:128, :] += right[128:256]
        rhs_ref[...] += left[128:136]
        spill_ref[128:136, :] += right[256:264]

    sweep(counts[0][0], lambda i: list_ref[i], recv_ref, add, bufs)


def inner_kernel(list_hbm, recv_ref, edge_band_ref, edge_rhs_ref, band_ref, rhs_ref, list_ref, list_sem, *bufs):
    list_copy = pltpu.make_async_copy(list_hbm, list_ref, list_sem)
    list_copy.start()
    slots = recv_ref.shape[0] * CAP
    last = band_ref.shape[0] - 1
    band_ref[0:last] = jnp.zeros((last, 2, 128, 128), F32)
    band_ref[last] = edge_band_ref[...]
    rhs_ref[...] = jnp.zeros_like(rhs_ref)
    rhs_ref[last:last + 1] = edge_rhs_ref[0:1, :]

    def add(word, out):
        at = ((word >> 8) & 255) - 1
        left, right = out
        band_ref[at, 0] += left[0:128]
        band_ref[at, 1] += right[0:128]
        band_ref[at + 1, 0] += right[128:256]
        rhs_ref[pl.ds(at, 1), :] += left[128:129]
        rhs_ref[pl.ds(at + 1, 1), :] += right[256:257]

    list_copy.wait()
    sweep(list_ref[slots + 1], lambda i: list_ref[slots - 1 - i], recv_ref, add, bufs)


def finish_kernel(band_ref, rhs_ref, spill_ref, band_hbm, rhs_hbm, first_band, first_rhs, sems):
    rest = pltpu.make_async_copy(band_ref.at[1:], band_hbm.at[1:], sems.at[0])
    lag = pltpu.make_async_copy(band_ref.at[0, 1], band_hbm.at[0, 1], sems.at[1])
    rest.start()
    lag.start()
    first_band[...] = band_ref[0, 0] + spill_ref[0:128, :]
    first_rhs[...] = rhs_ref[...]
    first_rhs[0:1, :] = rhs_ref[0:1, :] + spill_ref[128:129, :]
    diagonal = pltpu.make_async_copy(first_band, band_hbm.at[0, 0], sems.at[2])
    right = pltpu.make_async_copy(first_rhs, rhs_hbm, sems.at[3])
    diagonal.start()
    right.start()
    right.wait()
    diagonal.wait()
    lag.wait()
    rest.wait()


def buffers():
    return [
        pltpu.VMEM((2, 8, 128), F32),
        pltpu.VMEM((2, 64, 128), F32),
        pltpu.VMEM((272, 256), BF16),
        pltpu.VMEM((8, 128), F32),
    ] * GROUP


VMEM = pl.BlockSpec(memory_space=pltpu.VMEM)
SMEM = pl.BlockSpec(memory_space=pltpu.SMEM)
HBM = pl.BlockSpec(memory_space=pltpu.HBM)
SWEEP_COST = pl.CostEstimate(flops=4 << 30, bytes_accessed=4 << 20, transcendentals=0)


def edge(received):
    devices = received.shape[0]
    return pl.pallas_call(
        edge_kernel,
        out_shape=(
            jax.ShapeDtypeStruct((2, 128, 128), F32),
            jax.ShapeDtypeStruct((8, 128), F32),
            jax.ShapeDtypeStruct((136, 128), F32),
            jax.ShapeDtypeStruct((devices * CAP + 8,), jnp.int32),
        ),
        in_specs=[VMEM],
        out_specs=(VMEM, VMEM, VMEM, SMEM),
        scratch_shapes=[
            pltpu.VMEM((8, 128), jnp.int32),
            pltpu.SMEM((128,), jnp.int32),
            pltpu.SMEM((128,), jnp.int32),
            pltpu.SMEM((128,), jnp.int32),
            pltpu.SMEM((128,), jnp.int32),
            pltpu.SemaphoreType.DMA((4,)),
        ]
        + buffers(),
        compiler_params=pltpu.CompilerParams(vmem_limit_bytes=40 * MiB),
        cost_estimate=SWEEP_COST,
        name="edge",
    )(received)


def inner(lists, received, edge_band, edge_rhs):
    return pl.pallas_call(
        inner_kernel,
        out_shape=(
            jax.ShapeDtypeStruct((BLK_DEV, 2, 128, 128), F32),
            jax.ShapeDtypeStruct((BLK_DEV, 128), F32),
        ),
        in_specs=[HBM, VMEM, VMEM, VMEM],
        out_specs=(VMEM, VMEM),
        scratch_shapes=[pltpu.SMEM(lists.shape, jnp.int32), pltpu.SemaphoreType.DMA] + buffers(),
        compiler_params=pltpu.CompilerParams(vmem_limit_bytes=40 * MiB),
        cost_estimate=SWEEP_COST,
        name="inner",
    )(lists, received, edge_band, edge_rhs)


def finish(band, rhs, spill):
    return pl.pallas_call(
        finish_kernel,
        out_shape=(jax.ShapeDtypeStruct(band.shape, F32), jax.ShapeDtypeStruct(rhs.shape, F32)),
        in_specs=[VMEM, VMEM, VMEM],
        out_specs=(HBM, HBM),
        scratch_shapes=[
            pltpu.VMEM((128, 128), F32),
            pltpu.VMEM(rhs.shape, F32),
            pltpu.SemaphoreType.DMA((4,)),
        ],
        compiler_params=pltpu.CompilerParams(vmem_limit_bytes=16 * MiB),
        name="finish",
    )(band, rhs, spill)


def on_device(spline_index, spline_frac, projection, forces, row_owner, row_offset):
    device_count = lax.axis_size(AXES)
    sent = pack(row_owner[:, 0], row_offset, spline_index, spline_frac, projection, forces, device_count)
    received = lax.all_to_all(sent, AXES, split_axis=0, concat_axis=0, tiled=True)
    edge_band, edge_rhs, spill, lists = edge(received)
    route = [(i, (i + 1) % device_count) for i in range(device_count)]
    spill = lax.ppermute(spill, AXES, route)
    band, rhs = inner(lists, received, edge_band, edge_rhs)
    return finish(band, rhs, spill)


def solution(mesh):
    in_specs = (
        P(AXES, None, None, None),
        P(AXES, None, None, None),
        P(AXES, None, None, None),
        P(AXES, None),
        P(AXES, None),
        P(AXES),
    )
    out_specs = (P(AXES, None, None, None), P(AXES, None))
    return jax.shard_map(
        on_device, mesh=mesh, in_specs=in_specs, out_specs=out_specs, check_vma=False
    )
```
